32 devices in a mesh: tm: 16 (over z, y, x), lat: 2 (over core).
Axes of the slice: x: 2, y: 2, z: 4, core: 2. Of those that a mesh axis runs over, the one named last changes fastest.
Arguments:
- x_init: float32 [16, 5, 16, 1024], P('tm', None, 'lat'), may hold values from -6 to 6
- background: float32 [5, 16, 1024], P(None, 'lat'), may hold values from -6 to 6
- observed: float32 [16, 16, 1024], P('tm', 'lat'), may hold values from -6 to 6
- diff_lon: float32 [16, 16, 1024], P('tm', 'lat'), may hold values from 0.03 to 0.2
- diff_lat: float32 [16, 16, 1024], P('tm', 'lat'), may hold values from 0.03 to 0.2
- drift: float32 [16, 16, 1024], P('tm', 'lat'), may hold values from -0.3 to 0.3
- coupling: float32 [5, 5], replicated, may hold values from -0.4 to 0.4
- model_var: float32 [5], replicated, may hold values from 0.3 to 3
- obs_level: int32 [16, 16, 8], P('tm', 'lat'), may hold values from 0 to 4
- huber_class: int32 [16, 16, 8], P('tm', 'lat'), may hold values from 0 to 2
Outputs:
- state: float32 [16, 5, 16, 1024], P('tm', None, 'lat')
- multipliers: float32 [16, 5, 16, 1024], P('tm', None, 'lat')
- obs_multipliers: float32 [16, 16, 1024], P('tm', 'lat')
The draws below stay inside these ranges and needn't reach their ends.
All inputs are finite; a program needn't handle non-finite values.
Results may differ from the reference program's by a relative error of at most 0.0003.
Values sent between devices are 32-bit elements; how exact they have to be, the bound alone decides.
A program may use at most 64 MiB of HBM per device.

```python
import math
import jax
import jax.numpy as jnp
from jax import lax

LEVELS = 5
LONC = 1024
TILE = 128
STEPS = 4
ITERS = 2
NT = 16
NLAT = 16
NTILE = 8


def plant(result, own_key, low, top_value):
    longest = result.shape.index(max(result.shape))
    spots = []
    for shift in (0, 1):
        where = [jax.random.randint(jax.random.fold_in(own_key, axis), (), 0, length) for axis, length in enumerate(result.shape)]
        where[longest] = (where[longest] + shift) % result.shape[longest]
        spots.append(tuple(where))
    return result.at[spots[0]].set(low).at[spots[1]].set(top_value)


def block_levels(rng, extent, shards, low, high):
    def one(position, shards_of):
        draws = jax.random.uniform(jax.random.fold_in(jax.random.fold_in(rng, 6), position), (shards_of,), jnp.float32, low / len(shards), high / len(shards))
        return jnp.repeat(jnp.exp(draws), extent[position] // shards_of).reshape((-1,) + (1,) * (len(extent) - position - 1))

    loudness = one(*shards[0])
    for cut in shards[1:]:
        loudness = loudness * one(*cut)
    return loudness


def bell_draw(key, extent, scale, reach, cuts=(), kind=jnp.bfloat16):
    drawn = jax.random.normal(key, extent, jnp.float32) * scale
    if len(cuts) > 0:
        drawn = block_levels(key, extent, cuts, -0.22, 0.18) * drawn
    return jnp.clip(drawn, min=-reach, max=reach).astype(kind)


def setup_inputs(seed: int = 0) -> dict:
    streams_of = jax.random.split(jax.random.key(seed), 11)
    return {
        "x_init": bell_draw(streams_of[0], (NT, LEVELS, NLAT, LONC), 1.0, 6.0, ((0, 16), (2, 2)), jnp.float32),
        "background": bell_draw(streams_of[1], (LEVELS, NLAT, LONC), 1.0, 6.0, ((1, 2),), jnp.float32),
        "observed": bell_draw(streams_of[2], (NT, NLAT, LONC), 1.0, 6.0, ((0, 16), (1, 2)), jnp.float32),
        "diff_lon": jnp.clip(0.03 + 0.17 * jax.random.uniform(streams_of[3], (NT, NLAT, LONC), jnp.float32) ** block_levels(streams_of[3], (NT, NLAT, LONC), ((0, 16), (1, 2)), -0.2, 0.2), 0.03, 0.2),
        "diff_lat": jnp.clip(0.03 + 0.17 * jax.random.uniform(streams_of[4], (NT, NLAT, LONC), jnp.float32) ** block_levels(streams_of[4], (NT, NLAT, LONC), ((0, 16), (1, 2)), -0.2, 0.2), 0.03, 0.2),
        "drift": jnp.clip(jax.random.uniform(streams_of[5], (NT, NLAT, LONC), jnp.float32, -0.3, 0.3) * block_levels(streams_of[5], (NT, NLAT, LONC), ((0, 16), (1, 2)), -0.4, 0.0), -0.3, 0.3),
        "coupling": bell_draw(streams_of[6], (LEVELS, LEVELS), 0.1, 0.4, (), jnp.float32),
        "model_var": jnp.clip(jnp.exp(jax.random.uniform(streams_of[7], (LEVELS,), jnp.float32, math.log(0.3), math.log(3.0))), 0.3, 3.0),
        "obs_level": plant(jax.random.randint(streams_of[8], (NT, NLAT, NTILE), 0, LEVELS), jax.random.fold_in(streams_of[8], 1), 0, LEVELS - 1).astype(jnp.int32),
        "huber_class": plant(jax.random.randint(streams_of[9], (NT, NLAT, NTILE), 0, 3), jax.random.fold_in(streams_of[9], 1), 0, 2).astype(jnp.int32),
    }


def local_step(v, north, south, kx, ky, ux, coupling):
    east = jnp.roll(v, -1, 2)
    west = jnp.roll(v, 1, 2)
    mixed = jnp.einsum('lm,mrc->lrc', coupling, v, precision=lax.Precision.HIGHEST)
    return v + kx * (east + west - 2.0 * v) + ky * (north + south - 2.0 * v) + 0.5 * ux * (east - west) + mixed

def adjoint_local(w, qnorth, qsouth, kx, ky, ux, coupling):
    p_term = kx * w
    q_term = ky * w
    u_term = ux * w
    mixed = jnp.einsum('lm,lrc->mrc', coupling, w, precision=lax.Precision.HIGHEST)
    lon_part = jnp.roll(p_term, -1, 2) + jnp.roll(p_term, 1, 2) - 2.0 * p_term
    adv_part = 0.5 * (jnp.roll(u_term, 1, 2) - jnp.roll(u_term, -1, 2))
    return w + lon_part + qnorth + qsouth - 2.0 * q_term + adv_part + mixed

def forward_model(v, kx, ky, ux, coupling):
    for step in range(STEPS):
        padded = jnp.pad(v, ((0, 0), (1, 1), (0, 0)))
        v = local_step(v, padded[:, 2:], padded[:, :-2], kx, ky, ux, coupling)
    return v

def adjoint_model(w, kx, ky, ux, coupling):
    for step in range(STEPS):
        padded = jnp.pad(ky * w, ((0, 0), (1, 1), (0, 0)))
        w = adjoint_local(w, padded[:, 2:], padded[:, :-2], kx, ky, ux, coupling)
    return w

def level_table(obs_level):
    levels = jnp.arange(LEVELS, dtype=jnp.int32)
    return (obs_level[None] == levels[:, None, None]).astype(jnp.float32)

def sample(x, table):
    lev, rows, cols = x.shape
    pieces = x.reshape(lev, rows, cols // TILE, TILE) * table[..., None]
    return lax.optimization_barrier(jnp.sum(pieces, axis=0)).reshape(rows, cols)

def spread(field, table):
    rows, cols = field.shape
    pieces = table[..., None] * field.reshape(rows, cols // TILE, TILE)[None]
    return pieces.reshape(table.shape[0], rows, cols)

def huber_cells(huber_class):
    tiles = 1.0 * (huber_class == 0) + 0.5 * (huber_class == 1) + 0.25 * (huber_class == 2)
    tiles = tiles.astype(jnp.float32)
    rows, count = tiles.shape
    return (tiles[..., None] * jnp.ones((TILE,), jnp.float32)).reshape(rows, count * TILE)

def reference(x_init, background, observed, diff_lon, diff_lat, drift, coupling, model_var, obs_level, huber_class):
    tables = jax.vmap(level_table)(obs_level)
    weights = jax.vmap(huber_cells)(huber_class)
    run_forward = jax.vmap(forward_model, in_axes=(0, 0, 0, 0, None))
    run_adjoint = jax.vmap(adjoint_model, in_axes=(0, 0, 0, 0, None))
    state = x_init
    multipliers = jnp.zeros_like(x_init)
    obs_multipliers = jnp.zeros_like(observed)
    for it in range(ITERS):
        moved = run_forward(state, diff_lon, diff_lat, drift, coupling)
        prior = jnp.concatenate([background[None], moved[:-1]], axis=0)
        multipliers = multipliers + 0.5 * (state - prior - model_var[None, :, None, None] * multipliers)
        misfit = jax.vmap(sample)(state, tables) - observed
        obs_multipliers = obs_multipliers + 0.5 * (weights * misfit - obs_multipliers)
        later = jnp.concatenate([multipliers[1:], jnp.zeros_like(multipliers[:1])], axis=0)
        pulled = run_adjoint(later, diff_lon, diff_lat, drift, coupling)
        gradient = multipliers - pulled + jax.vmap(spread)(obs_multipliers, tables)
        scale = jnp.sqrt(jnp.sum(gradient * gradient) / gradient.size + 1e-06)
        state = state - 0.3 * gradient / scale
    return (state, multipliers, obs_multipliers)
```

```python
import functools

import jax
import jax.numpy as jnp
from jax import lax
from jax.experimental import pallas as pl
from jax.experimental.pallas import tpu as pltpu
from jax.sharding import PartitionSpec as P

TILE = 128
STEPS = 4
HALO = 4 * STEPS
SLOT = 2 * HALO
PER = TILE // SLOT
F32 = jnp.float32
MESH = pl.DeviceIdType.MESH


def offsets_for(groups):
    found, step = [], 1
    while step < groups:
        found.append(step)
        step *= 4
    return found


def rounds_for(groups):
    offsets, most = offsets_for(groups), 1
    for g in range(groups):
        dist, edge = {g: 0}, [g]
        for at in edge:
            for d in offsets:
                for t in (at - d, at + d):
                    if 0 <= t < groups and t not in dist:
                        dist[t] = dist[at] + 1
                        edge.append(t)
        most = max(most, max(dist.values()))
    return most


def kernel(
    subs,
    bands,
    per_group,
    x_hbm,
    bg_hbm,
    obs_hbm,
    kx_hbm,
    ky_hbm,
    ux_hbm,
    mix_hbm,
    var_hbm,
    lev_hbm,
    cls_hbm,
    xs,
    m1,
    om,
    g2,
    scale_out,
    raw,
    coupling,
    variance,
    lev_in,
    cls_in,
    levh,
    wgth,
    g1h,
    packs,
    hal,
    hnext,
    main,
    x,
    lam,
    lam2,
    gg,
    gg2,
    a1,
    a2,
    a3,
    a4,
    bb,
    kyp,
    coef,
    omt,
    wgt,
    lev,
    prior,
    prior2,
    gnext,
    bgv,
    bsrc,
    bhal,
    row1,
    row2,
    slots1,
    slots2,
    spare,
    load_sem,
    ssem,
    rsem,
    rx,
    rh,
    gsem,
):
    j = lax.axis_index("tm")
    b = lax.axis_index("lat")
    n = subs * bands
    gme = j * bands + b
    levels, rows, cols = xs.shape
    tiles = cols // TILE
    height = bands * rows
    groups = subs // per_group
    peers = per_group * bands
    grp = j // per_group
    sme = lax.rem(j, per_group)
    me = sme * bands + b
    nq = hal.shape[2]
    xq = hnext.shape[1]
    first_group, last_group = grp == 0, grp == groups - 1
    last = per_group - 1

    def remote(src, dst, ss, rs, dev):
        return pltpu.make_async_remote_copy(
            src_ref=src,
            dst_ref=dst,
            send_sem=ssem.at[ss],
            recv_sem=rs,
            device_id=dev,
            device_id_type=MESH,
        )

    def peer(o):
        d = lax.rem(me + o, peers)
        return d, d // bands, lax.rem(d, bands), {
            "tm": grp * per_group + d // bands,
            "lat": lax.rem(d, bands),
        }

    def drain(sem, count):
        part = spare.at[0:count]
        pltpu.make_async_copy(part, part, sem).wait()

    def arrived(ref, sem):
        pltpu.make_async_copy(ref, ref, sem).wait()

    def lanes(t):
        return pl.ds(pl.multiple_of(t * TILE, TILE), TILE)

    def band(p):
        return pl.ds(rows * p, rows)

    def padded(p, shift=0):
        return pl.ds(rows + rows * p + shift, rows)

    def zero(ref):
        ref[...] = jnp.zeros(ref.shape, F32)

    nxt = {"tm": lax.rem(j + per_group, subs)}
    prv = {"tm": lax.rem(j + subs - per_group, subs)}
    barrier = pltpu.get_barrier_semaphore()

    near = []
    for d in offsets_for(groups):
        near += [(grp >= d, j - d * per_group), (grp + d < groups, j + d * per_group)]
    greeted = sum(jnp.where(ok, 1, 0) for ok, _ in near) if near else 0

    def greet(sem):
        for ok, t in near:
            @pl.when(ok)
            def _():
                pl.semaphore_signal(sem, inc=1, device_id={"tm": t}, device_id_type=MESH)

    for o in range(1, peers):
        pl.semaphore_signal(barrier, inc=1, device_id=peer(o)[3], device_id_type=MESH)
    greet(barrier)

    loads = [
        pltpu.make_async_copy(s, d, load_sem.at[i])
        for i, (s, d) in enumerate(
            [
                (x_hbm.at[0], xs),
                (kx_hbm.at[0], raw.at[0]),
                (ky_hbm.at[0], raw.at[1]),
                (ux_hbm.at[0], raw.at[2]),
                (obs_hbm.at[0], raw.at[3]),
                (lev_hbm.at[0], lev_in),
                (cls_hbm.at[0], cls_in),
                (mix_hbm, coupling),
                (var_hbm, variance),
            ]
        )
    ]
    for c in loads:
        c.start()
    load_bg = pltpu.make_async_copy(bg_hbm, bgv, load_sem.at[9])

    @pl.when(first_group)
    def _():
        load_bg.start()

    def zero_edges(ref):
        edge = jnp.zeros(ref.shape[:-2] + (rows, TILE), F32)
        ref[(slice(None),) * (len(ref.shape) - 2) + (pl.ds(0, rows),)] = edge
        ref[(slice(None),) * (len(ref.shape) - 2) + (pl.ds(rows + height, rows),)] = edge

    for ref in (a1, bb, kyp):
        zero_edges(ref)

    pl.semaphore_wait(barrier, peers - 1 + greeted)

    own = lanes(me)
    mine = [pltpu.make_async_copy(x_hbm.at[0, :, :, own], x.at[sme, 0, :, band(b)], rx.at[sme])]
    fields = (kx_hbm, ky_hbm, ux_hbm, obs_hbm)
    mine += [
        pltpu.make_async_copy(f.at[0, :, own], main.at[i, sme, band(b)], rsem.at[0])
        for i, f in enumerate(fields)
    ]
    for o in range(1, peers):
        d, _, _, dev = peer(o)
        remote(x_hbm.at[0, :, :, lanes(d)], x.at[sme, 0, :, band(b)], 0, rx.at[sme], dev).start()
    for o in range(1, peers):
        d, _, _, dev = peer(o)
        for i, f in enumerate(fields):
            remote(f.at[0, :, lanes(d)], main.at[i, sme, band(b)], 0, rsem.at[0], dev).start()
    for c in mine:
        c.start()

    lane = lax.broadcasted_iota(jnp.int32, (rows, TILE), 1)
    lane_first, lane_last = lane == 0, lane == TILE - 1
    right_side = lane < HALO
    inside = jnp.logical_or(right_side, lane >= TILE - HALO)
    place = lax.rem(lane + HALO, TILE) // SLOT

    def join(parts):
        out = parts[0]
        for k in range(1, len(parts)):
            out = jnp.where(place == k, parts[k], out)
        return out

    def turn(a, k):
        return a if k == 0 else pltpu.roll(a, SLOT * k, 1)

    def at(t):
        t = t % tiles
        return slice(t * TILE, (t + 1) * TILE)

    for c in loads:
        c.wait()

    for t in range(tiles):
        lev_t = jnp.broadcast_to(lev_in[:, t : t + 1], (rows, TILE))
        k = jnp.broadcast_to(cls_in[:, t : t + 1], (rows, TILE))
        levh[:, at(t)] = lev_t.astype(F32)
        wgth[:, at(t)] = jnp.where(
            k == 0, 1.0, jnp.where(k == 1, 0.5, jnp.where(k == 2, 0.25, 0.0))
        ).astype(F32)

    def field(f, t):
        if f < levels:
            return xs[f, :, at(t)]
        if f < levels + 4:
            return raw[f - levels, :, at(t)]
        return (wgth if f == levels + 4 else levh)[:, at(t)]

    count = levels + 6
    for q in range(nq):
        held = range(q * PER, min((q + 1) * PER, count))
        moved = [[turn(field(f, t), f - q * PER) for f in held] for t in range(tiles)]
        for d in range(tiles):
            parts = []
            for i, f in enumerate(held):
                side = jnp.logical_and(lane >= SLOT * i, lane < SLOT * i + HALO)
                parts.append(
                    jnp.where(side, moved[(d + 1) % tiles][i], moved[(d - 1) % tiles][i])
                )
            if q * PER <= count < (q + 1) * PER:
                parts.append(
                    jnp.where(
                        lax.rem(lane + HALO, SLOT) < HALO, wgth[:, at(d)], levh[:, at(d)]
                    )
                )
            packs[d, q] = join(parts)

    for o in range(1, peers):
        d, _, _, dev = peer(o)
        remote(packs.at[d], hal.at[sme, b], 0, rh.at[sme], dev).start()
    pltpu.make_async_copy(packs.at[me], hal.at[sme, b], rh.at[sme]).start()

    @pl.when(first_group)
    def _():
        load_bg.wait()
        for o in range(bands):
            e = lax.rem(b + o, bands)
            d = sme * bands + e
            lo, hi = lanes(lax.rem(d + tiles - 1, tiles)), lanes(lax.rem(d + 1, tiles))
            for q in range(xq):
                bsrc[o, q] = join(
                    [
                        turn(jnp.where(right_side, bgv[l, :, hi], bgv[l, :, lo]), l - q * PER)
                        for l in range(q * PER, min((q + 1) * PER, levels))
                    ]
                )
            src = bg_hbm.at[:, :, lanes(d)]
            if o == 0:
                pltpu.make_async_copy(src, prior.at[0, :, band(b)], rsem.at[1]).start()
                pltpu.make_async_copy(bsrc.at[0], bhal.at[b], rsem.at[2]).start()
            else:
                remote(src, prior.at[0, :, band(b)], 1, rsem.at[1], {"lat": e}).start()
                remote(bsrc.at[o], bhal.at[b], 1, rsem.at[2], {"lat": e}).start()
        zero(prior2)

    @pl.when(last_group)
    def _():
        zero(x.at[per_group])
        zero(gnext)

    def pick(get, choice):
        out = jnp.where(choice == 0.0, get(0), 0.0)
        for l in range(1, levels):
            out += jnp.where(choice == float(l), get(l), 0.0)
        return out

    for t in range(tiles):
        miss = pick(lambda l: xs[l, :, at(t)], levh[:, at(t)]) - raw[3, :, at(t)]
        om[:, at(t)] = 0.5 * (wgth[:, at(t)] * miss)

    arrived(x.at[0, 0], rx.at[0])
    arrived(hal.at[0], rh.at[0])

    @pl.when(jnp.logical_not(first_group))
    def _():
        remote(x.at[0, 0], x.at[per_group, 0], 2, rsem.at[3], prv).start()
        remote(hal.at[0, :, 0:xq], hnext, 2, rsem.at[4], prv).start()

    for s in range(1, per_group):
        arrived(x.at[s, 0], rx.at[s])
        arrived(hal.at[s], rh.at[s])
    arrived(main, rsem.at[0])

    def unpack(ref, f):
        return jnp.where(inside, turn(ref[f // PER], (PER - f % PER) % PER), 0.0)

    def column(a, c):
        return jnp.broadcast_to(a[:, c : c + 1], (rows, TILE))

    for s in range(per_group):
        for p in range(bands):
            got = hal.at[s, p]
            for l in range(levels):
                x[s, 1, l, band(p)] = unpack(got, l)
            for t in range(2):
                kx, ky, ux, ob = (
                    main[i, s, band(p)] if t == 0 else unpack(got, levels + i) for i in range(4)
                )
                coef[0, s, t, band(p)] = 1.0 - 2.0 * kx - 2.0 * ky
                coef[1, s, t, band(p)] = kx + 0.5 * ux
                coef[2, s, t, band(p)] = kx - 0.5 * ux
                kyp[s, t, padded(p)] = ky
                omt[s, t, band(p)] = ob
            wgt[s, 1, band(p)] = unpack(got, levels + 4)
            lev[s, 1, band(p)] = unpack(got, levels + 5)
            info = got[count // PER]
            base = SLOT * (count % PER)
            wgt[s, 0, band(p)] = column(info, (base + TILE - HALO) % TILE)
            lev[s, 0, band(p)] = column(info, base)

    def east(a, after):
        return pltpu.roll(jnp.where(lane_first, after, a), TILE - 1, 1)

    def west(a, before):
        return pltpu.roll(jnp.where(lane_last, before, a), 1, 1)

    mix = [[coupling[l, m] for m in range(levels)] for l in range(levels)]

    def step(src, dst, s, p, adjoint):
        v = [[src[s, t, l, padded(p)] for l in range(levels)] for t in range(2)]
        for t in range(2):
            cc = coef[0, s, t, band(p)]
            ce, cw = (coef[k + 2 * adjoint, s, t, band(p)] for k in (1, 2))
            if adjoint:
                cu, cd = kyp[s, t, padded(p, 1)], kyp[s, t, padded(p, -1)]
            else:
                cr = kyp[s, t, padded(p)]
            for l in range(levels):
                a, o = v[t][l], v[1 - t][l]
                up, down = src[s, t, l, padded(p, 1)], src[s, t, l, padded(p, -1)]
                out = cc * a
                for m in range(levels):
                    out += (mix[m][l] if adjoint else mix[l][m]) * v[t][m]
                if adjoint:
                    out += cu * up
                    out += cd * down
                else:
                    out += cr * (up + down)
                out += ce * east(a, o)
                out += cw * west(a, o)
                dst[s, t, l, padded(p)] = out

    def apply(buf, which, adjoint):
        if not which:
            return

        def body(_, carry):
            for src, dst in ((buf, bb), (bb, buf)):
                for s in which:
                    for p in range(bands):
                        step(src, dst, s, p, adjoint)
            return carry

        lax.fori_loop(0, STEPS // 2, body, 0)

    def every(which=(0, 1)):
        return [(t, l, p) for t in which for l in range(levels) for p in range(bands)]

    for s in range(per_group):
        for t, l, p in every():
            a1[s, t, l, padded(p)] = x[s, t, l, band(p)]

    apply(a1, [last], False)

    @pl.when(jnp.logical_not(last_group))
    def _():
        for t in range(2):
            remote(
                a1.at[last, t, :, pl.ds(rows, height)], prior.at[t], 3, rsem.at[5], nxt
            ).start()

    apply(a1, list(range(last)), False)

    for s in range(per_group):
        for p in range(bands):
            for t in range(2):
                coef[3, s, t, band(p)] = east(*(coef[2, s, k, band(p)] for k in (t, 1 - t)))
                coef[4, s, t, band(p)] = west(*(coef[1, s, k, band(p)] for k in (t, 1 - t)))
                miss = pick(lambda l: x[s, t, l, band(p)], lev[s, t, band(p)])
                omt[s, t, band(p)] = 0.5 * (wgt[s, t, band(p)] * (miss - omt[s, t, band(p)]))
    for ref in (a2, a3, a4):
        zero_edges(ref)

    for r in range(rounds_for(groups) if near else 0):
        greet(gsem.at[r])
        pl.semaphore_wait(gsem.at[r], greeted)

    for s in range(last):
        for t, l, p in every():
            val = 0.5 * (x[s + 1, t, l, band(p)] - a1[s, t, l, padded(p)])
            lam[s + 1, t, l, band(p)] = val
            a2[s, t, l, padded(p)] = val
    apply(a2, list(range(last)), True)

    @pl.when(jnp.logical_not(last_group))
    def _():
        arrived(x.at[per_group, 0], rsem.at[3])
        arrived(hnext, rsem.at[4])
        for l in range(levels):
            for p in range(bands):
                x[per_group, 1, l, band(p)] = unpack(hnext.at[p], l)

    has_later = jnp.where(last_group, 0.0, 1.0).astype(F32)
    for t, l, p in every():
        val = (0.5 * has_later) * (x[per_group, t, l, band(p)] - a1[last, t, l, padded(p)])
        lam[per_group, t, l, band(p)] = val
        a2[last, t, l, padded(p)] = val
    apply(a2, [last], True)

    @pl.when(first_group)
    def _():
        arrived(prior.at[0], rsem.at[1])
        arrived(bhal, rsem.at[2])
        for l in range(levels):
            for p in range(bands):
                prior[1, l, band(p)] = unpack(bhal.at[p], l)

    @pl.when(jnp.logical_not(first_group))
    def _():
        arrived(prior, rsem.at[5])

    for t, l, p in every():
        lam[0, t, l, band(p)] = 0.5 * (x[0, t, l, band(p)] - prior[t, l, band(p)])

    total = jnp.zeros((rows, TILE), F32)
    for s in range(per_group):
        for t, l, p in every():
            grad = lam[s, t, l, band(p)] - a2[s, t, l, padded(p)]
            grad += jnp.where(lev[s, t, band(p)] == float(l), omt[s, t, band(p)], 0.0)
            gg[s, t, l, band(p)] = grad
            a3[s, t, l, padded(p)] = grad
            if t == 0:
                total += grad * grad
        if s == 0:
            @pl.when(jnp.logical_not(first_group))
            def _():
                remote(gg.at[0], gnext, 4, rsem.at[6], prv).start()

    row1[...] = jnp.sum(total, axis=0, keepdims=True)

    def share(src, slots, k):
        def body(o, carry):
            t = lax.rem(gme + o, n)
            dev = {"tm": t // bands, "lat": lax.rem(t, bands)}
            remote(src, slots.at[o - 1], 9 + k, rsem.at[11 + k], dev).start()
            return carry

        lax.fori_loop(1, n, body, 0)

    def gathered(row, slots, k):
        arrived(slots, rsem.at[11 + k])
        full = jnp.sum(row[...] + jnp.sum(slots[...], axis=0), axis=1, keepdims=True)
        size = float(levels * rows * cols * n)
        return 0.3 / jnp.sqrt(full / size + 1e-6)

    def home(src, dst, k):
        for o in range(1, peers):
            _, s, p, dev = peer(o)
            remote(
                src(s, pl.ds(pl.multiple_of(p * rows, rows), rows)),
                dst.at[:, :, own],
                6 + k,
                rsem.at[8 + k],
                dev,
            ).start()
        pltpu.make_async_copy(
            src(sme, pl.ds(pl.multiple_of(b * rows, rows), rows)), dst.at[:, :, own], rsem.at[8 + k]
        ).start()

    share(row1, slots1, 0)
    home(lambda s, r: gg.at[s, 0, :, r], g1h, 0)

    apply(a3, [last], False)

    @pl.when(jnp.logical_not(last_group))
    def _():
        for t in range(2):
            remote(
                a3.at[last, t, :, pl.ds(rows, height)], prior2.at[t], 5, rsem.at[7], nxt
            ).start()

    apply(a3, list(range(last)), False)

    c1 = gathered(row1, slots1, 0)
    h1 = 0.5 * c1

    def second(s, t, l, r, q):
        return (2.0 - 0.5 * variance[l]) * lam[s, t, l, r] - h1 * q

    for s in range(last):
        for t, l, p in every():
            q = gg[s + 1, t, l, band(p)] - a3[s, t, l, padded(p)]
            val = second(s + 1, t, l, band(p), q)
            a4[s, t, l, padded(p)] = val
            if t == 0:
                lam2[s + 1, l, band(p)] = val
    apply(a4, list(range(last)), True)

    @pl.when(jnp.logical_not(last_group))
    def _():
        arrived(gnext, rsem.at[6])

    for t, l, p in every():
        q = gnext[t, l, band(p)] - a3[last, t, l, padded(p)]
        val = second(per_group, t, l, band(p), has_later * q)
        a4[last, t, l, padded(p)] = val

    @pl.when(jnp.logical_not(first_group))
    def _():
        arrived(prior2, rsem.at[7])

    for _, l, p in every((0,)):
        q = gg[0, 0, l, band(p)] - prior2[0, l, band(p)]
        lam2[0, l, band(p)] = second(0, 0, l, band(p), q)
    home(lambda s, r: lam2.at[s, :, r], m1, 1)

    apply(a4, [last], True)

    total = jnp.zeros((rows, TILE), F32)
    for s in range(per_group):
        for p in range(bands):
            where = lev[s, 0, band(p)]
            seen = pick(lambda l: gg[s, 0, l, band(p)], where)
            om2 = 1.5 * omt[s, 0, band(p)] - h1 * (wgt[s, 0, band(p)] * seen)
            for l in range(levels):
                grad = lam2[s, l, band(p)] - a4[s, 0, l, padded(p)]
                grad += jnp.where(where == float(l), om2, 0.0)
                gg2[s, l, band(p)] = grad
                total += grad * grad
    row2[...] = jnp.sum(total, axis=0, keepdims=True)
    share(row2, slots2, 1)
    home(lambda s, r: gg2.at[s, :, r], g2, 2)

    arrived(g1h, rsem.at[8])
    for l in range(levels):
        xs[l] = xs[l] - c1 * g1h[l]
    for t in range(tiles):
        miss = pick(lambda l: xs[l, :, at(t)], levh[:, at(t)]) - raw[3, :, at(t)]
        om[:, at(t)] += 0.5 * (wgth[:, at(t)] * miss - om[:, at(t)])

    drain(ssem.at[0], (peers - 1) * (levels + 4 + nq))
    for k in range(3):
        drain(ssem.at[6 + k], (peers - 1) * levels)

    @pl.when(first_group)
    def _():
        if bands > 1:
            drain(ssem.at[1], (bands - 1) * (levels + xq))

    @pl.when(jnp.logical_not(first_group))
    def _():
        drain(ssem.at[2], bands * (levels + xq))
        drain(ssem.at[4], bands * 2 * levels)

    @pl.when(jnp.logical_not(last_group))
    def _():
        drain(ssem.at[3], bands * 2 * levels)
        drain(ssem.at[5], bands * 2 * levels)

    arrived(slots1, ssem.at[9])
    arrived(slots2, ssem.at[10])
    arrived(m1, rsem.at[9])
    arrived(g2, rsem.at[10])
    scale_out[...] = jnp.broadcast_to(gathered(row2, slots2, 1), (1, TILE))


def finish(x, mult, om, grad, scale, state_out, mult_out, om_out, state, sem):
    copies = [
        pltpu.make_async_copy(mult, mult_out.at[0], sem.at[0]),
        pltpu.make_async_copy(om, om_out.at[0], sem.at[1]),
    ]
    for c in copies:
        c.start()
    s = scale[0:1, 0:1]
    for l in range(x.shape[0]):
        state[l] = x[l] - s * grad[l]
    copies.append(pltpu.make_async_copy(state, state_out.at[0], sem.at[2]))
    copies[2].start()
    for c in copies:
        c.wait()


def on_device(subs, bands, *args):
    x = args[0]
    _, levels, rows, cols = x.shape
    n = subs * bands
    tiles = cols // TILE
    per_group = tiles // bands
    if per_group * bands != tiles or subs % per_group:
        raise ValueError("unsupported mesh")
    groups = subs // per_group
    height = bands * rows
    nq = -(-(levels + 7) // PER)
    xq = -(-levels // PER)
    dma = pltpu.SemaphoreType.DMA
    vm = lambda *shape: pltpu.VMEM(shape, F32)
    full = vm(levels, rows, cols)
    cell = vm(rows, cols)
    small = pltpu.VMEM((rows, tiles), jnp.int32)
    anywhere = pl.BlockSpec(memory_space=pltpu.HBM)
    vmem = pl.BlockSpec(memory_space=pltpu.VMEM)
    wide = vm(per_group, 2, levels, height + 2 * rows, TILE)
    pair = vm(2, levels, height, TILE)
    held = pl.pallas_call(
        functools.partial(kernel, subs, bands, per_group),
        out_shape=(full, full, cell, full, vm(1, TILE)),
        in_specs=[anywhere] * 10,
        out_specs=(vmem,) * 5,
        scratch_shapes=[
            vm(4, rows, cols),
            pltpu.SMEM((levels, levels), F32),
            pltpu.SMEM((levels,), F32),
            small,
            small,
            cell,
            cell,
            full,
            vm(tiles, nq, rows, TILE),
            vm(per_group, bands, nq, rows, TILE),
            vm(bands, xq, rows, TILE),
            vm(4, per_group, height, TILE),
            vm(per_group + 1, 2, levels, height, TILE),
            vm(per_group + 1, 2, levels, height, TILE),
            vm(per_group, levels, height, TILE),
            vm(per_group, 2, levels, height, TILE),
            vm(per_group, levels, height, TILE),
            wide,
            wide,
            wide,
            wide,
            wide,
            vm(per_group, 2, height + 2 * rows, TILE),
            vm(5, per_group, 2, height, TILE),
            vm(per_group, 2, height, TILE),
            vm(per_group, 2, height, TILE),
            vm(per_group, 2, height, TILE),
            pair,
            pair,
            pair,
            full,
            vm(bands, xq, rows, TILE),
            vm(bands, xq, rows, TILE),
            vm(1, TILE),
            vm(1, TILE),
            vm(n - 1, 1, TILE),
            vm(n - 1, 1, TILE),
            vm(max((tiles - 1) * (levels + 4 + nq), 2 * bands * levels), rows, TILE),
            dma((10,)),
            dma((11,)),
            dma((13,)),
            dma((per_group,)),
            dma((per_group,)),
            pltpu.SemaphoreType.REGULAR((rounds_for(groups),)),
        ],
        compiler_params=pltpu.CompilerParams(
            collective_id=0,
            has_side_effects=True,
        ),
    )(*args)
    return pl.pallas_call(
        finish,
        out_shape=(
            jax.ShapeDtypeStruct(x.shape, F32),
            jax.ShapeDtypeStruct(x.shape, F32),
            jax.ShapeDtypeStruct((1, rows, cols), F32),
        ),
        in_specs=[vmem] * 5,
        out_specs=(anywhere,) * 3,
        scratch_shapes=[full, dma((3,))],
        compiler_params=pltpu.CompilerParams(vmem_limit_bytes=16 << 20),
    )(*held)


def solution(mesh):
    placed = (
        P("tm", None, "lat", None),
        P(None, "lat", None),
        P("tm", "lat", None),
        P("tm", "lat", None),
        P("tm", "lat", None),
        P("tm", "lat", None),
        P(),
        P(),
        P("tm", "lat", None),
        P("tm", "lat", None),
    )
    return jax.shard_map(
        functools.partial(on_device, mesh.shape["tm"], mesh.shape["lat"]),
        mesh=mesh,
        in_specs=placed,
        out_specs=(P("tm", None, "lat", None), P("tm", None, "lat", None), P("tm", "lat", None)),
        check_vma=False,
    )
```

```python
import functools

import jax
import jax.numpy as jnp
from jax import lax
from jax.experimental import pallas as pl
from jax.experimental.pallas import tpu as pltpu
from jax.sharding import PartitionSpec as P

TILE = 128
STEPS = 4
HALO = 4 * STEPS
SLOT = 2 * HALO
PER = TILE // SLOT
F32 = jnp.float32
MESH = pl.DeviceIdType.MESH


def offsets_for(groups):
    found, step = [], 1
    while step < groups:
        found.append(step)
        step *= 4
    return found


def rounds_for(groups):
    offsets, most = offsets_for(groups), 1
    for g in range(groups):
        dist, edge = {g: 0}, [g]
        for at in edge:
            for d in offsets:
                for t in (at - d, at + d):
                    if 0 <= t < groups and t not in dist:
                        dist[t] = dist[at] + 1
                        edge.append(t)
        most = max(most, max(dist.values()))
    return most


def kernel(
    subs,
    bands,
    per_group,
    x_hbm,
    bg_hbm,
    obs_hbm,
    kx_hbm,
    ky_hbm,
    ux_hbm,
    mix_hbm,
    var_hbm,
    lev_hbm,
    cls_hbm,
    xs,
    m1,
    om,
    g2,
    scale_out,
    raw,
    coupling,
    variance,
    lev_in,
    cls_in,
    levh,
    wgth,
    lamh,
    g1h,
    qh,
    packs,
    late,
    hal,
    hlate,
    hnext,
    main,
    x,
    lam,
    qm,
    gg,
    gg2,
    a1,
    a2,
    a3,
    a4,
    a5,
    bb,
    kyp,
    coef,
    omt,
    wgt,
    lev,
    prior,
    prior2,
    gnext,
    bgv,
    bsrc,
    bhal,
    ghal,
    psend,
    gsend,
    row1,
    row2,
    slots1,
    slots2,
    spare,
    load_sem,
    ssem,
    rsem,
    rx,
    rh,
    gsem,
):
    j = lax.axis_index("tm")
    b = lax.axis_index("lat")
    n = subs * bands
    gme = j * bands + b
    levels, rows, cols = xs.shape
    tiles = cols // TILE
    height = bands * rows
    groups = subs // per_group
    peers = per_group * bands
    grp = j // per_group
    sme = lax.rem(j, per_group)
    me = sme * bands + b
    nq = hal.shape[2]
    nl = hlate.shape[2]
    xq = hnext.shape[1]
    first_group, last_group = grp == 0, grp == groups - 1
    last = per_group - 1

    def remote(src, dst, ss, rs, dev):
        return pltpu.make_async_remote_copy(
            src_ref=src,
            dst_ref=dst,
            send_sem=ssem.at[ss],
            recv_sem=rs,
            device_id=dev,
            device_id_type=MESH,
        )

    def peer(o):
        d = lax.rem(me + o, peers)
        return d, d // bands, lax.rem(d, bands), {
            "tm": grp * per_group + d // bands,
            "lat": lax.rem(d, bands),
        }

    def drain(sem, count):
        part = spare.at[0:count]
        pltpu.make_async_copy(part, part, sem).wait()

    def arrived(ref, sem):
        pltpu.make_async_copy(ref, ref, sem).wait()

    def lanes(t):
        return pl.ds(pl.multiple_of(t * TILE, TILE), TILE)

    def band(p):
        return pl.ds(rows * p, rows)

    def padded(p, shift=0):
        return pl.ds(rows + rows * p + shift, rows)

    def zero(ref):
        ref[...] = jnp.zeros(ref.shape, F32)

    nxt = {"tm": lax.rem(j + per_group, subs)}
    prv = {"tm": lax.rem(j + subs - per_group, subs)}
    barrier = pltpu.get_barrier_semaphore()

    near = []
    for d in offsets_for(groups):
        near += [(grp >= d, j - d * per_group), (grp + d < groups, j + d * per_group)]
    greeted = sum(jnp.where(ok, 1, 0) for ok, _ in near) if near else 0

    def greet(sem):
        for ok, t in near:
            @pl.when(ok)
            def _():
                pl.semaphore_signal(sem, inc=1, device_id={"tm": t}, device_id_type=MESH)

    for o in range(1, peers):
        pl.semaphore_signal(barrier, inc=1, device_id=peer(o)[3], device_id_type=MESH)
    greet(barrier)

    loads = [
        pltpu.make_async_copy(s, d, load_sem.at[i])
        for i, (s, d) in enumerate(
            [
                (x_hbm.at[0], xs),
                (kx_hbm.at[0], raw.at[0]),
                (ky_hbm.at[0], raw.at[1]),
                (ux_hbm.at[0], raw.at[2]),
                (obs_hbm.at[0], raw.at[3]),
                (lev_hbm.at[0], lev_in),
                (cls_hbm.at[0], cls_in),
                (mix_hbm, coupling),
                (var_hbm, variance),
            ]
        )
    ]
    for c in loads:
        c.start()
    load_bg = pltpu.make_async_copy(bg_hbm, bgv, load_sem.at[9])

    @pl.when(first_group)
    def _():
        load_bg.start()

    def zero_edges(ref):
        edge = jnp.zeros(ref.shape[:-2] + (rows, TILE), F32)
        ref[(slice(None),) * (len(ref.shape) - 2) + (pl.ds(0, rows),)] = edge
        ref[(slice(None),) * (len(ref.shape) - 2) + (pl.ds(rows + height, rows),)] = edge

    for ref in (a1, bb, kyp):
        zero_edges(ref)

    pl.semaphore_wait(barrier, peers - 1 + greeted)

    told = []

    def tell():
        if near and len(told) < rounds_for(groups):
            greet(gsem.at[len(told)])
            told.append(False)

    def heard(upto):
        for r in range(upto + 1):
            if not told[r]:
                pl.semaphore_wait(gsem.at[r], greeted)
                told[r] = True

    def pass_on():
        heard(len(told) - 1)
        tell()

    tell()

    own = lanes(me)
    fields = (kx_hbm, ky_hbm, ux_hbm)
    pltpu.make_async_copy(
        x_hbm.at[0, :, :, own], x.at[sme, 0, :, band(b)], rx.at[sme]
    ).start()
    for o in range(1, peers):
        d, _, _, dev = peer(o)
        remote(x_hbm.at[0, :, :, lanes(d)], x.at[sme, 0, :, band(b)], 0, rx.at[sme], dev).start()
    for i, f in enumerate(fields):
        pltpu.make_async_copy(f.at[0, :, own], main.at[i, sme, band(b)], rsem.at[0]).start()
    for o in range(1, peers):
        d, _, _, dev = peer(o)
        for i, f in enumerate(fields):
            remote(f.at[0, :, lanes(d)], main.at[i, sme, band(b)], 0, rsem.at[0], dev).start()

    lane = lax.broadcasted_iota(jnp.int32, (rows, TILE), 1)
    lane_first, lane_last = lane == 0, lane == TILE - 1
    right_side = lane < HALO
    inside = jnp.logical_or(right_side, lane >= TILE - HALO)
    place = lax.rem(lane + HALO, TILE) // SLOT

    def join(parts):
        out = parts[0]
        for k in range(1, len(parts)):
            out = jnp.where(place == k, parts[k], out)
        return out

    def turn(a, k):
        return a if k == 0 else pltpu.roll(a, SLOT * k, 1)

    def at(t):
        t = t % tiles
        return slice(t * TILE, (t + 1) * TILE)

    for c in loads:
        c.wait()

    for t in range(tiles):
        lev_t = jnp.broadcast_to(lev_in[:, t : t + 1], (rows, TILE))
        k = jnp.broadcast_to(cls_in[:, t : t + 1], (rows, TILE))
        levh[:, at(t)] = lev_t.astype(F32)
        wgth[:, at(t)] = jnp.where(
            k == 0, 1.0, jnp.where(k == 1, 0.5, jnp.where(k == 2, 0.25, 0.0))
        ).astype(F32)

    def field(f, t):
        if f < levels:
            return xs[f, :, at(t)]
        if f < levels + 4:
            return raw[f - levels, :, at(t)]
        return (wgth if f == levels + 4 else levh)[:, at(t)]

    def pack(dst, q, held, extra=None):
        moved = [[turn(field(f, t), i) for i, f in enumerate(held)] for t in range(tiles)]
        for d in range(tiles):
            parts = []
            for i in range(len(held)):
                side = jnp.logical_and(lane >= SLOT * i, lane < SLOT * i + HALO)
                parts.append(
                    jnp.where(side, moved[(d + 1) % tiles][i], moved[(d - 1) % tiles][i])
                )
            if extra is not None:
                parts.append(extra(d))
            dst[d, q] = join(parts)

    early = levels + 3
    for q in range(nq):
        pack(packs, q, range(q * PER, min((q + 1) * PER, early)))
    for o in range(1, peers):
        d, _, _, dev = peer(o)
        remote(packs.at[d], hal.at[sme, b], 0, rh.at[sme], dev).start()
    pltpu.make_async_copy(packs.at[me], hal.at[sme, b], rh.at[sme]).start()

    front = lax.rem(lane + HALO, SLOT) < HALO
    pack(
        late,
        0,
        range(early, early + 3),
        lambda d: jnp.where(front, wgth[:, at(d)], levh[:, at(d)]),
    )
    pltpu.make_async_copy(obs_hbm.at[0, :, own], main.at[3, sme, band(b)], rsem.at[14]).start()
    pltpu.make_async_copy(late.at[me], hlate.at[sme, b], rsem.at[17]).start()
    for o in range(1, peers):
        d, _, _, dev = peer(o)
        remote(obs_hbm.at[0, :, lanes(d)], main.at[3, sme, band(b)], 0, rsem.at[14], dev).start()
        remote(late.at[d], hlate.at[sme, b], 0, rsem.at[17], dev).start()

    pass_on()

    @pl.when(first_group)
    def _():
        load_bg.wait()
        for o in range(bands):
            e = lax.rem(b + o, bands)
            d = sme * bands + e
            lo, hi = lanes(lax.rem(d + tiles - 1, tiles)), lanes(lax.rem(d + 1, tiles))
            for q in range(xq):
                bsrc[o, q] = join(
                    [
                        turn(jnp.where(right_side, bgv[l, :, hi], bgv[l, :, lo]), l - q * PER)
                        for l in range(q * PER, min((q + 1) * PER, levels))
                    ]
                )
            src = bg_hbm.at[:, :, lanes(d)]
            if o == 0:
                pltpu.make_async_copy(src, prior.at[0, :, band(b)], rsem.at[1]).start()
                pltpu.make_async_copy(bsrc.at[0], bhal.at[b], rsem.at[2]).start()
            else:
                remote(src, prior.at[0, :, band(b)], 1, rsem.at[1], {"lat": e}).start()
                remote(bsrc.at[o], bhal.at[b], 1, rsem.at[2], {"lat": e}).start()
        zero(prior2)

    @pl.when(last_group)
    def _():
        zero(x.at[per_group])
        zero(gnext)

    def pick(get, choice):
        out = jnp.where(choice == 0.0, get(0), 0.0)
        for l in range(1, levels):
            out += jnp.where(choice == float(l), get(l), 0.0)
        return out

    for t in range(tiles):
        miss = pick(lambda l: xs[l, :, at(t)], levh[:, at(t)]) - raw[3, :, at(t)]
        om[:, at(t)] = 0.5 * (wgth[:, at(t)] * miss)

    arrived(x.at[0, 0], rx.at[0])

    @pl.when(jnp.logical_not(first_group))
    def _():
        remote(x.at[0, 0], x.at[per_group, 0], 2, rsem.at[3], prv).start()

    arrived(hal.at[0], rh.at[0])

    @pl.when(jnp.logical_not(first_group))
    def _():
        remote(hal.at[0, :, 0:xq], hnext, 2, rsem.at[4], prv).start()

    pass_on()

    for s in range(1, per_group):
        arrived(x.at[s, 0], rx.at[s])
        arrived(hal.at[s], rh.at[s])
    arrived(main.at[0:3], rsem.at[0])

    def unpack(ref, f):
        return jnp.where(inside, turn(ref[f // PER], (PER - f % PER) % PER), 0.0)

    def column(a, c):
        return jnp.broadcast_to(a[:, c : c + 1], (rows, TILE))

    def prepare(s):
        for p in range(bands):
            got = hal.at[s, p]
            for l in range(levels):
                a1[s, 0, l, padded(p)] = x[s, 0, l, band(p)]
                val = unpack(got, l)
                x[s, 1, l, band(p)] = val
                a1[s, 1, l, padded(p)] = val
            for t in range(2):
                kx, ky, ux = (
                    main[i, s, band(p)] if t == 0 else unpack(got, levels + i) for i in range(3)
                )
                coef[0, s, t, band(p)] = 1.0 - 2.0 * kx - 2.0 * ky
                coef[1, s, t, band(p)] = kx + 0.5 * ux
                coef[2, s, t, band(p)] = kx - 0.5 * ux
                kyp[s, t, padded(p)] = ky

    def prepare_late(s):
        for p in range(bands):
            for t in range(2):
                coef[3, s, t, band(p)] = east(*(coef[2, s, k, band(p)] for k in (t, 1 - t)))
                coef[4, s, t, band(p)] = west(*(coef[1, s, k, band(p)] for k in (t, 1 - t)))
            got = hlate.at[s, p]
            wgt[s, 1, band(p)] = unpack(got, 1)
            lev[s, 1, band(p)] = unpack(got, 2)
            info = got[3 // PER]
            base = SLOT * (3 % PER)
            wgt[s, 0, band(p)] = column(info, (base + TILE - HALO) % TILE)
            lev[s, 0, band(p)] = column(info, base)
            for t in range(2):
                ob = main[3, s, band(p)] if t == 0 else unpack(got, 0)
                miss = pick(lambda l: x[s, t, l, band(p)], lev[s, t, band(p)]) - ob
                omt[s, t, band(p)] = 0.5 * (wgt[s, t, band(p)] * miss)

    def east(a, after):
        return pltpu.roll(jnp.where(lane_first, after, a), TILE - 1, 1)

    def west(a, before):
        return pltpu.roll(jnp.where(lane_last, before, a), 1, 1)

    mix = [[coupling[l, m] for m in range(levels)] for l in range(levels)]

    def step(src, dst, s, p, adjoint):
        v = [[src[s, t, l, padded(p)] for l in range(levels)] for t in range(2)]
        for t in range(2):
            cc = coef[0, s, t, band(p)]
            ce, cw = (coef[k + 2 * adjoint, s, t, band(p)] for k in (1, 2))
            if adjoint:
                cu, cd = kyp[s, t, padded(p, 1)], kyp[s, t, padded(p, -1)]
            else:
                cr = kyp[s, t, padded(p)]
            for l in range(levels):
                a, o = v[t][l], v[1 - t][l]
                up, down = src[s, t, l, padded(p, 1)], src[s, t, l, padded(p, -1)]
                out = cc * a
                for m in range(levels):
                    out += (mix[m][l] if adjoint else mix[l][m]) * v[t][m]
                if adjoint:
                    out += cu * up
                    out += cd * down
                else:
                    out += cr * (up + down)
                out += ce * east(a, o)
                out += cw * west(a, o)
                dst[s, t, l, padded(p)] = out

    def apply(buf, which, adjoint):
        if not which:
            return

        def body(_, carry):
            for src, dst in ((buf, bb), (bb, buf)):
                for s in which:
                    for p in range(bands):
                        step(src, dst, s, p, adjoint)
            return carry

        lax.fori_loop(0, STEPS // 2, body, 0)

    def every(which=(0, 1)):
        return [(t, l, p) for t in which for l in range(levels) for p in range(bands)]

    def squeeze(dst, get):
        for p in range(bands):
            for q in range(xq):
                dst[p, q] = join(
                    [turn(get(l, p), l - q * PER) for l in range(q * PER, min((q + 1) * PER, levels))]
                )

    def widen(dst, src):
        for l in range(levels):
            for p in range(bands):
                dst[1, l, band(p)] = unpack(src.at[p], l)

    def home(src, dst, k, wanted=None):
        for o in range(1, peers):
            _, s, p, dev = peer(o)

            def send():
                remote(
                    src(s, pl.ds(pl.multiple_of(p * rows, rows), rows)),
                    dst.at[:, :, own],
                    6 + k,
                    rsem.at[8 + k],
                    dev,
                ).start()

            if wanted is None:
                send()
            else:
                pl.when(wanted(s))(send)

        def keep():
            mine = src(sme, pl.ds(pl.multiple_of(b * rows, rows), rows))
            pltpu.make_async_copy(mine, dst.at[:, :, own], rsem.at[8 + k]).start()

        if wanted is None:
            keep()
        else:
            pl.when(wanted(sme))(keep)

    def share(src, slots, k):
        def body(t, carry):
            o = lax.rem(t + n - gme, n)

            @pl.when(o > 0)
            def _():
                dev = {"tm": t // bands, "lat": lax.rem(t, bands)}
                remote(src, slots.at[o - 1], 10 + k, rsem.at[12 + k], dev).start()

            return carry

        lax.fori_loop(0, n, body, 0)

    def gathered(row, slots, k):
        arrived(slots, rsem.at[12 + k])
        full = jnp.sum(row[...] + jnp.sum(slots[...], axis=0), axis=1, keepdims=True)
        size = float(levels * rows * cols * n)
        return 0.3 / jnp.sqrt(full / size + 1e-6)

    rest = list(range(last))

    prepare(last)
    apply(a1, [last], False)

    @pl.when(jnp.logical_not(last_group))
    def _():
        remote(a1.at[last, 0, :, pl.ds(rows, height)], prior.at[0], 3, rsem.at[5], nxt).start()
        squeeze(psend, lambda l, p: a1[last, 1, l, padded(p)])
        remote(psend, bhal, 3, rsem.at[15], nxt).start()

    for s in rest:
        prepare(s)
    apply(a1, rest, False)

    arrived(main.at[3], rsem.at[14])
    arrived(hlate, rsem.at[17])
    for s in range(per_group):
        prepare_late(s)
    for ref in (a2, a3, a4, a5):
        zero_edges(ref)

    def first_adjoint(s, val, t, l, p):
        lam[s + 1, t, l, band(p)] = val
        a2[s, t, l, padded(p)] = val
        a5[s, t, l, padded(p)] = (2.0 - 0.5 * variance[l]) * val

    for s in rest:
        for t, l, p in every():
            val = 0.5 * (x[s + 1, t, l, band(p)] - a1[s, t, l, padded(p)])
            first_adjoint(s, val, t, l, p)
    home(lambda s, r: lam.at[s, 0, :, r], lamh, 0, lambda s: s > 0)
    apply(a2, rest, True)

    while near and len(told) < rounds_for(groups):
        pass_on()
    heard(len(told) - 1)

    @pl.when(jnp.logical_not(last_group))
    def _():
        arrived(x.at[per_group, 0], rsem.at[3])
        arrived(hnext, rsem.at[4])
        widen(x.at[per_group], hnext)

    has_later = jnp.where(last_group, 0.0, 1.0).astype(F32)
    for t, l, p in every():
        val = (0.5 * has_later) * (x[per_group, t, l, band(p)] - a1[last, t, l, padded(p)])
        first_adjoint(last, val, t, l, p)
    apply(a2, [last], True)

    def gradient(s, total):
        for t, l, p in every():
            grad = lam[s, t, l, band(p)] - a2[s, t, l, padded(p)]
            grad += jnp.where(lev[s, t, band(p)] == float(l), omt[s, t, band(p)], 0.0)
            gg[s, t, l, band(p)] = grad
            a3[s, t, l, padded(p)] = grad
            if t == 0:
                total += grad * grad
        return total

    def prior_lam():
        @pl.when(first_group)
        def _():
            arrived(prior.at[0], rsem.at[1])
            arrived(bhal, rsem.at[2])

        @pl.when(jnp.logical_not(first_group))
        def _():
            arrived(prior.at[0], rsem.at[5])
            arrived(bhal, rsem.at[15])

        widen(prior, bhal)
        for t, l, p in every():
            lam[0, t, l, band(p)] = 0.5 * (x[0, t, l, band(p)] - prior[t, l, band(p)])

    def send_first():
        @pl.when(jnp.logical_not(first_group))
        def _():
            remote(gg.at[0, 0], gnext.at[0], 4, rsem.at[6], prv).start()
            squeeze(gsend, lambda l, p: gg[0, 1, l, band(p)])
            remote(gsend, ghal, 4, rsem.at[16], prv).start()

    def send_last():
        @pl.when(jnp.logical_not(last_group))
        def _():
            remote(
                a3.at[last, 0, :, pl.ds(rows, height)], prior2, 5, rsem.at[7], nxt
            ).start()

    total = jnp.zeros((rows, TILE), F32)
    if last > 0:
        for s in range(1, per_group):
            total = gradient(s, total)
        apply(a3, [last], False)
        send_last()
    prior_lam()
    total = gradient(0, total)
    row1[...] = jnp.sum(total, axis=0, keepdims=True)
    send_first()
    share(row1, slots1, 0)
    home(lambda s, r: lam.at[s, 0, :, r], lamh, 0, lambda s: s == 0)
    home(lambda s, r: gg.at[s, 0, :, r], g1h, 1)
    if last > 0:
        apply(a3, rest, False)
    else:
        apply(a3, [last], False)
        send_last()

    apply(a5, list(range(per_group)), True)

    for s in rest:
        for t, l, p in every():
            q = gg[s + 1, t, l, band(p)] - a3[s, t, l, padded(p)]
            a4[s, t, l, padded(p)] = q
            if t == 0:
                qm[s + 1, l, band(p)] = q

    @pl.when(jnp.logical_not(first_group))
    def _():
        arrived(prior2, rsem.at[7])

    for _, l, p in every((0,)):
        qm[0, l, band(p)] = gg[0, 0, l, band(p)] - prior2[l, band(p)]
    home(lambda s, r: qm.at[s, :, r], qh, 2)
    apply(a4, rest, True)

    @pl.when(jnp.logical_not(last_group))
    def _():
        arrived(gnext.at[0], rsem.at[6])
        arrived(ghal, rsem.at[16])
        widen(gnext, ghal)

    for t, l, p in every():
        q = gnext[t, l, band(p)] - a3[last, t, l, padded(p)]
        a4[last, t, l, padded(p)] = has_later * q
    apply(a4, [last], True)

    c1 = gathered(row1, slots1, 0)
    h1 = 0.5 * c1

    total = jnp.zeros((rows, TILE), F32)
    for s in range(per_group):
        for p in range(bands):
            where = lev[s, 0, band(p)]
            seen = pick(lambda l: gg[s, 0, l, band(p)], where)
            om2 = 1.5 * omt[s, 0, band(p)] - h1 * (wgt[s, 0, band(p)] * seen)
            for l in range(levels):
                plain = (2.0 - 0.5 * variance[l]) * lam[s, 0, l, band(p)] - a5[s, 0, l, padded(p)]
                grad = plain - h1 * (qm[s, l, band(p)] - a4[s, 0, l, padded(p)])
                grad += jnp.where(where == float(l), om2, 0.0)
                gg2[s, l, band(p)] = grad
                total += grad * grad
    row2[...] = jnp.sum(total, axis=0, keepdims=True)
    share(row2, slots2, 1)
    home(lambda s, r: gg2.at[s, :, r], g2, 3)

    arrived(g1h, rsem.at[9])
    for l in range(levels):
        xs[l] = xs[l] - c1 * g1h[l]
    for t in range(tiles):
        miss = pick(lambda l: xs[l, :, at(t)], levh[:, at(t)]) - raw[3, :, at(t)]
        om[:, at(t)] += 0.5 * (wgth[:, at(t)] * miss - om[:, at(t)])
    arrived(lamh, rsem.at[8])
    arrived(qh, rsem.at[10])
    for l in range(levels):
        m1[l] = (2.0 - 0.5 * variance[l]) * lamh[l] - h1 * qh[l]

    drain(ssem.at[0], (peers - 1) * (levels + 4 + nq + nl))
    for k in range(4):
        drain(ssem.at[6 + k], (peers - 1) * levels)

    @pl.when(first_group)
    def _():
        if bands > 1:
            drain(ssem.at[1], (bands - 1) * (levels + xq))

    @pl.when(jnp.logical_not(first_group))
    def _():
        drain(ssem.at[2], bands * (levels + xq))
        drain(ssem.at[4], bands * (levels + xq))

    @pl.when(jnp.logical_not(last_group))
    def _():
        drain(ssem.at[3], bands * (levels + xq))
        drain(ssem.at[5], bands * levels)

    arrived(slots1, ssem.at[10])
    arrived(slots2, ssem.at[11])
    arrived(g2, rsem.at[11])
    scale_out[...] = jnp.broadcast_to(gathered(row2, slots2, 1), (1, TILE))


def finish(x, mult, om, grad, scale, state_out, mult_out, om_out, state, sem):
    copies = [
        pltpu.make_async_copy(mult, mult_out.at[0], sem.at[0]),
        pltpu.make_async_copy(om, om_out.at[0], sem.at[1]),
    ]
    for c in copies:
        c.start()
    s = scale[0:1, 0:1]
    for l in range(x.shape[0]):
        state[l] = x[l] - s * grad[l]
    copies.append(pltpu.make_async_copy(state, state_out.at[0], sem.at[2]))
    copies[2].start()
    for c in copies:
        c.wait()


def on_device(subs, bands, *args):
    x = args[0]
    _, levels, rows, cols = x.shape
    n = subs * bands
    tiles = cols // TILE
    per_group = tiles // bands
    if per_group * bands != tiles or subs % per_group:
        raise ValueError("unsupported mesh")
    groups = subs // per_group
    height = bands * rows
    nq = -(-(levels + 3) // PER)
    nl = -(-4 // PER)
    xq = -(-levels // PER)
    dma = pltpu.SemaphoreType.DMA
    vm = lambda *shape: pltpu.VMEM(shape, F32)
    full = vm(levels, rows, cols)
    cell = vm(rows, cols)
    small = pltpu.VMEM((rows, tiles), jnp.int32)
    anywhere = pl.BlockSpec(memory_space=pltpu.HBM)
    vmem = pl.BlockSpec(memory_space=pltpu.VMEM)
    wide = vm(per_group, 2, levels, height + 2 * rows, TILE)
    pair = vm(2, levels, height, TILE)
    held = pl.pallas_call(
        functools.partial(kernel, subs, bands, per_group),
        out_shape=(full, full, cell, full, vm(1, TILE)),
        in_specs=[anywhere] * 10,
        out_specs=(vmem,) * 5,
        scratch_shapes=[
            vm(4, rows, cols),
            pltpu.SMEM((levels, levels), F32),
            pltpu.SMEM((levels,), F32),
            small,
            small,
            cell,
            cell,
            full,
            full,
            full,
            vm(tiles, nq, rows, TILE),
            vm(tiles, nl, rows, TILE),
            vm(per_group, bands, nq, rows, TILE),
            vm(per_group, bands, nl, rows, TILE),
            vm(bands, xq, rows, TILE),
            vm(4, per_group, height, TILE),
            vm(per_group + 1, 2, levels, height, TILE),
            vm(per_group + 1, 2, levels, height, TILE),
            vm(per_group, levels, height, TILE),
            vm(per_group, 2, levels, height, TILE),
            vm(per_group, levels, height, TILE),
            wide,
            wide,
            wide,
            wide,
            wide,
            wide,
            vm(per_group, 2, height + 2 * rows, TILE),
            vm(5, per_group, 2, height, TILE),
            vm(per_group, 2, height, TILE),
            vm(per_group, 2, height, TILE),
            vm(per_group, 2, height, TILE),
            pair,
            vm(levels, height, TILE),
            pair,
            full,
            vm(bands, xq, rows, TILE),
            vm(bands, xq, rows, TILE),
            vm(bands, xq, rows, TILE),
            vm(bands, xq, rows, TILE),
            vm(bands, xq, rows, TILE),
            vm(1, TILE),
            vm(1, TILE),
            vm(n - 1, 1, TILE),
            vm(n - 1, 1, TILE),
            vm((tiles - 1) * (levels + 4 + nq + nl), rows, TILE),
            dma((10,)),
            dma((12,)),
            dma((18,)),
            dma((per_group,)),
            dma((per_group,)),
            pltpu.SemaphoreType.REGULAR((rounds_for(groups),)),
        ],
        compiler_params=pltpu.CompilerParams(
            collective_id=0,
            has_side_effects=True,
        ),
    )(*args)
    return pl.pallas_call(
        finish,
        out_shape=(
            jax.ShapeDtypeStruct(x.shape, F32),
            jax.ShapeDtypeStruct(x.shape, F32),
            jax.ShapeDtypeStruct((1, rows, cols), F32),
        ),
        in_specs=[vmem] * 5,
        out_specs=(anywhere,) * 3,
        scratch_shapes=[full, dma((3,))],
        compiler_params=pltpu.CompilerParams(vmem_limit_bytes=16 << 20),
    )(*held)


def solution(mesh):
    placed = (
        P("tm", None, "lat", None),
        P(None, "lat", None),
        P("tm", "lat", None),
        P("tm", "lat", None),
        P("tm", "lat", None),
        P("tm", "lat", None),
        P(),
        P(),
        P("tm", "lat", None),
        P("tm", "lat", None),
    )
    return jax.shard_map(
        functools.partial(on_device, mesh.shape["tm"], mesh.shape["lat"]),
        mesh=mesh,
        in_specs=placed,
        out_specs=(P("tm", None, "lat", None), P("tm", None, "lat", None), P("tm", "lat", None)),
        check_vma=False,
    )
```

```python
import functools

import jax
import jax.numpy as jnp
from jax import lax
from jax.experimental import pallas as pl
from jax.experimental.pallas import tpu as pltpu
from jax.sharding import PartitionSpec as P

TILE = 128
STEPS = 4
HALO = 4 * STEPS
SLOT = 2 * HALO
PER = TILE // SLOT
F32 = jnp.float32
MESH = pl.DeviceIdType.MESH


def offsets_for(groups):
    found, step = [], 1
    while step < groups:
        found.append(step)
        step *= 4
    return found


def rounds_for(groups):
    offsets, most = offsets_for(groups), 1
    for g in range(groups):
        dist, edge = {g: 0}, [g]
        for at in edge:
            for d in offsets:
                for t in (at - d, at + d):
                    if 0 <= t < groups and t not in dist:
                        dist[t] = dist[at] + 1
                        edge.append(t)
        most = max(most, max(dist.values()))
    return most


def kernel(
    subs,
    bands,
    per_group,
    x_hbm,
    bg_hbm,
    obs_hbm,
    kx_hbm,
    ky_hbm,
    ux_hbm,
    mix_hbm,
    var_hbm,
    lev_hbm,
    cls_hbm,
    xs,
    m1,
    om,
    g2,
    scale_out,
    raw,
    coupling,
    variance,
    lev_in,
    cls_in,
    levh,
    wgth,
    lamh,
    g1h,
    qh,
    packs,
    late,
    hal,
    hlate,
    hnext,
    main,
    x,
    lam,
    qm,
    gg,
    first,
    second,
    third,
    a1,
    a2,
    a3,
    a4,
    a5,
    bb,
    kyp,
    centre,
    coef,
    omt,
    wgt,
    lev,
    prior,
    prior2,
    gnext,
    bgv,
    bsrc,
    bhal,
    ghal,
    psend,
    gsend,
    row1,
    row2,
    slots1,
    slots2,
    spare,
    load_sem,
    ssem,
    rsem,
    rx,
    rh,
    gsem,
):
    j = lax.axis_index("tm")
    b = lax.axis_index("lat")
    n = subs * bands
    gme = j * bands + b
    levels, rows, cols = xs.shape
    tiles = cols // TILE
    height = bands * rows
    groups = subs // per_group
    peers = per_group * bands
    grp = j // per_group
    sme = lax.rem(j, per_group)
    me = sme * bands + b
    nq = hal.shape[2]
    nl = hlate.shape[2]
    xq = hnext.shape[1]
    first_group, last_group = grp == 0, grp == groups - 1
    last = per_group - 1

    def remote(src, dst, ss, rs, dev):
        return pltpu.make_async_remote_copy(
            src_ref=src,
            dst_ref=dst,
            send_sem=ssem.at[ss],
            recv_sem=rs,
            device_id=dev,
            device_id_type=MESH,
        )

    def peer(o):
        d = lax.rem(me + o, peers)
        return d, d // bands, lax.rem(d, bands), {
            "tm": grp * per_group + d // bands,
            "lat": lax.rem(d, bands),
        }

    def drain(sem, count):
        part = spare.at[0:count]
        pltpu.make_async_copy(part, part, sem).wait()

    def arrived(ref, sem):
        pltpu.make_async_copy(ref, ref, sem).wait()

    def lanes(t):
        return pl.ds(pl.multiple_of(t * TILE, TILE), TILE)

    def band(p):
        return pl.ds(rows * p, rows)

    def padded(p, shift=0):
        return pl.ds(rows + rows * p + shift, rows)

    def zero(ref):
        ref[...] = jnp.zeros(ref.shape, F32)

    nxt = {"tm": lax.rem(j + per_group, subs)}
    prv = {"tm": lax.rem(j + subs - per_group, subs)}
    barrier = pltpu.get_barrier_semaphore()

    near = []
    for d in offsets_for(groups):
        near += [(grp >= d, j - d * per_group), (grp + d < groups, j + d * per_group)]
    greeted = sum(jnp.where(ok, 1, 0) for ok, _ in near) if near else 0

    def greet(sem):
        for ok, t in near:
            @pl.when(ok)
            def _():
                pl.semaphore_signal(sem, inc=1, device_id={"tm": t}, device_id_type=MESH)

    for o in range(1, peers):
        pl.semaphore_signal(barrier, inc=1, device_id=peer(o)[3], device_id_type=MESH)
    greet(barrier)

    loads = [
        pltpu.make_async_copy(s, d, load_sem.at[i])
        for i, (s, d) in enumerate(
            [
                (x_hbm.at[0], xs),
                (kx_hbm.at[0], raw.at[0]),
                (ky_hbm.at[0], raw.at[1]),
                (ux_hbm.at[0], raw.at[2]),
                (obs_hbm.at[0], raw.at[3]),
                (lev_hbm.at[0], lev_in),
                (cls_hbm.at[0], cls_in),
                (mix_hbm, coupling),
                (var_hbm, variance),
            ]
        )
    ]
    for c in loads:
        c.start()
    load_bg = pltpu.make_async_copy(bg_hbm, bgv, load_sem.at[9])

    @pl.when(first_group)
    def _():
        load_bg.start()

    def zero_edges(ref):
        edge = jnp.zeros(ref.shape[:-2] + (rows, TILE), F32)
        ref[(slice(None),) * (len(ref.shape) - 2) + (pl.ds(0, rows),)] = edge
        ref[(slice(None),) * (len(ref.shape) - 2) + (pl.ds(rows + height, rows),)] = edge

    for ref in (a1, bb, kyp):
        zero_edges(ref)

    pl.semaphore_wait(barrier, peers - 1 + greeted)

    told = []

    def tell():
        if near and len(told) < rounds_for(groups):
            greet(gsem.at[len(told)])
            told.append(False)

    def heard(upto):
        for r in range(upto + 1):
            if not told[r]:
                pl.semaphore_wait(gsem.at[r], greeted)
                told[r] = True

    def pass_on():
        heard(len(told) - 1)
        tell()

    tell()

    own = lanes(me)
    fields = (kx_hbm, ky_hbm, ux_hbm)
    pltpu.make_async_copy(
        x_hbm.at[0, :, :, own], x.at[sme, 0, :, band(b)], rx.at[sme]
    ).start()
    for o in range(1, peers):
        d, _, _, dev = peer(o)
        remote(x_hbm.at[0, :, :, lanes(d)], x.at[sme, 0, :, band(b)], 0, rx.at[sme], dev).start()
    for i, f in enumerate(fields):
        pltpu.make_async_copy(f.at[0, :, own], main.at[i, sme, band(b)], rsem.at[0]).start()
    for o in range(1, peers):
        d, _, _, dev = peer(o)
        for i, f in enumerate(fields):
            remote(f.at[0, :, lanes(d)], main.at[i, sme, band(b)], 0, rsem.at[0], dev).start()

    lane = lax.broadcasted_iota(jnp.int32, (rows, TILE), 1)
    lane_first, lane_last = lane == 0, lane == TILE - 1
    right_side = lane < HALO
    inside = jnp.logical_or(right_side, lane >= TILE - HALO)
    place = lax.rem(lane + HALO, TILE) // SLOT

    def join(parts):
        out = parts[0]
        for k in range(1, len(parts)):
            out = jnp.where(place == k, parts[k], out)
        return out

    def turn(a, k):
        return a if k == 0 else pltpu.roll(a, SLOT * k, 1)

    def at(t):
        t = t % tiles
        return slice(t * TILE, (t + 1) * TILE)

    for c in loads:
        c.wait()

    for t in range(tiles):
        lev_t = jnp.broadcast_to(lev_in[:, t : t + 1], (rows, TILE))
        k = jnp.broadcast_to(cls_in[:, t : t + 1], (rows, TILE))
        levh[:, at(t)] = lev_t.astype(F32)
        wgth[:, at(t)] = jnp.where(
            k == 0, 1.0, jnp.where(k == 1, 0.5, jnp.where(k == 2, 0.25, 0.0))
        ).astype(F32)

    def field(f, t):
        if f < levels:
            return xs[f, :, at(t)]
        if f < levels + 4:
            return raw[f - levels, :, at(t)]
        return (wgth if f == levels + 4 else levh)[:, at(t)]

    def pack(dst, q, held, extra=None):
        moved = [[turn(field(f, t), i) for i, f in enumerate(held)] for t in range(tiles)]
        for d in range(tiles):
            parts = []
            for i in range(len(held)):
                side = jnp.logical_and(lane >= SLOT * i, lane < SLOT * i + HALO)
                parts.append(
                    jnp.where(side, moved[(d + 1) % tiles][i], moved[(d - 1) % tiles][i])
                )
            if extra is not None:
                parts.append(extra(d))
            dst[d, q] = join(parts)

    early = levels + 3
    for q in range(nq):
        pack(packs, q, range(q * PER, min((q + 1) * PER, early)))
    for o in range(1, peers):
        d, _, _, dev = peer(o)
        remote(packs.at[d], hal.at[sme, b], 0, rh.at[sme], dev).start()
    pltpu.make_async_copy(packs.at[me], hal.at[sme, b], rh.at[sme]).start()

    front = lax.rem(lane + HALO, SLOT) < HALO
    pack(
        late,
        0,
        range(early, early + 3),
        lambda d: jnp.where(front, wgth[:, at(d)], levh[:, at(d)]),
    )
    pltpu.make_async_copy(obs_hbm.at[0, :, own], main.at[3, sme, band(b)], rsem.at[15]).start()
    pltpu.make_async_copy(late.at[me], hlate.at[sme, b], rsem.at[18]).start()
    for o in range(1, peers):
        d, _, _, dev = peer(o)
        remote(obs_hbm.at[0, :, lanes(d)], main.at[3, sme, band(b)], 0, rsem.at[15], dev).start()
        remote(late.at[d], hlate.at[sme, b], 0, rsem.at[18], dev).start()

    pass_on()

    @pl.when(first_group)
    def _():
        load_bg.wait()
        for o in range(bands):
            e = lax.rem(b + o, bands)
            d = sme * bands + e
            lo, hi = lanes(lax.rem(d + tiles - 1, tiles)), lanes(lax.rem(d + 1, tiles))
            for q in range(xq):
                bsrc[o, q] = join(
                    [
                        turn(jnp.where(right_side, bgv[l, :, hi], bgv[l, :, lo]), l - q * PER)
                        for l in range(q * PER, min((q + 1) * PER, levels))
                    ]
                )
            src = bg_hbm.at[:, :, lanes(d)]
            if o == 0:
                pltpu.make_async_copy(src, prior.at[0, :, band(b)], rsem.at[1]).start()
                pltpu.make_async_copy(bsrc.at[0], bhal.at[b], rsem.at[2]).start()
            else:
                remote(src, prior.at[0, :, band(b)], 1, rsem.at[1], {"lat": e}).start()
                remote(bsrc.at[o], bhal.at[b], 1, rsem.at[2], {"lat": e}).start()
        zero(prior2)

    @pl.when(last_group)
    def _():
        zero(x.at[per_group])
        zero(gnext)

    def pick(get, choice):
        out = jnp.where(choice == 0.0, get(0), 0.0)
        for l in range(1, levels):
            out += jnp.where(choice == float(l), get(l), 0.0)
        return out

    for t in range(tiles):
        miss = pick(lambda l: xs[l, :, at(t)], levh[:, at(t)]) - raw[3, :, at(t)]
        om[:, at(t)] = 0.5 * (wgth[:, at(t)] * miss)

    arrived(x.at[0, 0], rx.at[0])

    @pl.when(jnp.logical_not(first_group))
    def _():
        remote(x.at[0, 0], x.at[per_group, 0], 2, rsem.at[3], prv).start()

    arrived(hal.at[0], rh.at[0])

    @pl.when(jnp.logical_not(first_group))
    def _():
        remote(hal.at[0, :, 0:xq], hnext, 2, rsem.at[4], prv).start()

    pass_on()

    for s in range(1, per_group):
        arrived(x.at[s, 0], rx.at[s])
        arrived(hal.at[s], rh.at[s])
    arrived(main.at[0:3], rsem.at[0])

    def unpack(ref, f):
        return jnp.where(inside, turn(ref[f // PER], (PER - f % PER) % PER), 0.0)

    def column(a, c):
        return jnp.broadcast_to(a[:, c : c + 1], (rows, TILE))

    mix = [[coupling[l, m] for m in range(levels)] for l in range(levels)]

    def prepare(s):
        for p in range(bands):
            got = hal.at[s, p]
            for l in range(levels):
                a1[s, 0, l, padded(p)] = x[s, 0, l, band(p)]
                val = unpack(got, l)
                x[s, 1, l, band(p)] = val
                a1[s, 1, l, padded(p)] = val
            for t in range(2):
                kx, ky, ux = (
                    main[i, s, band(p)] if t == 0 else unpack(got, levels + i) for i in range(3)
                )
                plain = 1.0 - 2.0 * kx - 2.0 * ky
                for l in range(levels):
                    centre[l, s, t, band(p)] = plain + mix[l][l]
                coef[1, s, t, band(p)] = kx + 0.5 * ux
                coef[2, s, t, band(p)] = kx - 0.5 * ux
                kyp[s, t, padded(p)] = ky

    def prepare_late(s):
        for p in range(bands):
            for t in range(2):
                coef[3, s, t, band(p)] = east(*(coef[2, s, k, band(p)] for k in (t, 1 - t)))
                coef[4, s, t, band(p)] = west(*(coef[1, s, k, band(p)] for k in (t, 1 - t)))
            got = hlate.at[s, p]
            wgt[s, 1, band(p)] = unpack(got, 1)
            lev[s, 1, band(p)] = unpack(got, 2)
            info = got[3 // PER]
            base = SLOT * (3 % PER)
            wgt[s, 0, band(p)] = column(info, (base + TILE - HALO) % TILE)
            lev[s, 0, band(p)] = column(info, base)
            for t in range(2):
                ob = main[3, s, band(p)] if t == 0 else unpack(got, 0)
                miss = pick(lambda l: x[s, t, l, band(p)], lev[s, t, band(p)]) - ob
                omt[s, t, band(p)] = 0.5 * (wgt[s, t, band(p)] * miss)

    def east(a, after):
        return pltpu.roll(jnp.where(lane_first, after, a), TILE - 1, 1)

    def west(a, before):
        return pltpu.roll(jnp.where(lane_last, before, a), 1, 1)

    def step(src, dst, s, p, adjoint):
        v = [[src[s, t, l, padded(p)] for l in range(levels)] for t in range(2)]
        for t in range(2):
            ce, cw = (coef[k + 2 * adjoint, s, t, band(p)] for k in (1, 2))
            if adjoint:
                cu, cd = kyp[s, t, padded(p, 1)], kyp[s, t, padded(p, -1)]
            else:
                cr = kyp[s, t, padded(p)]
            for l in range(levels):
                a, o = v[t][l], v[1 - t][l]
                up, down = src[s, t, l, padded(p, 1)], src[s, t, l, padded(p, -1)]
                out = centre[l, s, t, band(p)] * a
                for m in range(levels):
                    if m != l:
                        out += (mix[m][l] if adjoint else mix[l][m]) * v[t][m]
                if adjoint:
                    out += cu * up
                    out += cd * down
                else:
                    out += cr * (up + down)
                out += ce * east(a, o)
                out += cw * west(a, o)
                dst[s, t, l, padded(p)] = out

    def apply(buf, which, adjoint):
        if not which:
            return

        def body(_, carry):
            for src, dst in ((buf, bb), (bb, buf)):
                for s in which:
                    for p in range(bands):
                        step(src, dst, s, p, adjoint)
            return carry

        lax.fori_loop(0, STEPS // 2, body, 0)

    def every(which=(0, 1)):
        return [(t, l, p) for t in which for l in range(levels) for p in range(bands)]

    def squeeze(dst, get):
        for p in range(bands):
            for q in range(xq):
                dst[p, q] = join(
                    [turn(get(l, p), l - q * PER) for l in range(q * PER, min((q + 1) * PER, levels))]
                )

    def widen(dst, src):
        for l in range(levels):
            for p in range(bands):
                dst[1, l, band(p)] = unpack(src.at[p], l)

    def home(src, dst, k, wanted=None):
        for o in range(1, peers):
            _, s, p, dev = peer(o)

            def send():
                remote(
                    src(s, pl.ds(pl.multiple_of(p * rows, rows), rows)),
                    dst.at[:, :, own],
                    6 + k,
                    rsem.at[8 + k],
                    dev,
                ).start()

            if wanted is None:
                send()
            else:
                pl.when(wanted(s))(send)

        def keep():
            mine = src(sme, pl.ds(pl.multiple_of(b * rows, rows), rows))
            pltpu.make_async_copy(mine, dst.at[:, :, own], rsem.at[8 + k]).start()

        if wanted is None:
            keep()
        else:
            pl.when(wanted(sme))(keep)

    def share(src, slots, k):
        def body(t, carry):
            o = lax.rem(t + n - gme, n)

            @pl.when(o > 0)
            def _():
                dev = {"tm": t // bands, "lat": t % bands}
                remote(src, slots.at[o - 1], 11 + k, rsem.at[13 + k], dev).start()

            return carry

        if n > 64:
            lax.fori_loop(0, n, body, 0)
        else:
            for t in range(n):
                body(t, 0)

    def gathered(row, slots, k):
        arrived(slots, rsem.at[13 + k])
        full = jnp.sum(row[...] + jnp.sum(slots[...], axis=0), axis=1, keepdims=True)
        size = float(levels * rows * cols * n)
        return 0.3 / jnp.sqrt(full / size + 1e-6)

    rest = list(range(last))

    prepare(last)
    apply(a1, [last], False)

    @pl.when(jnp.logical_not(last_group))
    def _():
        remote(a1.at[last, 0, :, pl.ds(rows, height)], prior.at[0], 3, rsem.at[5], nxt).start()
        squeeze(psend, lambda l, p: a1[last, 1, l, padded(p)])
        remote(psend, bhal, 3, rsem.at[16], nxt).start()

    for s in rest:
        prepare(s)
    apply(a1, rest, False)

    arrived(main.at[3], rsem.at[15])
    arrived(hlate, rsem.at[18])
    for s in range(per_group):
        prepare_late(s)
    for ref in (a2, a3, a4, a5):
        zero_edges(ref)

    def later_apply(buf):
        @pl.when(jnp.logical_not(last_group))
        def _():
            apply(buf, [last], True)

    def first_adjoint(s, val, t, l, p):
        lam[s + 1, t, l, band(p)] = val
        a2[s, t, l, padded(p)] = val
        a5[s, t, l, padded(p)] = (2.0 - 0.5 * variance[l]) * val

    for s in rest:
        for t, l, p in every():
            val = 0.5 * (x[s + 1, t, l, band(p)] - a1[s, t, l, padded(p)])
            first_adjoint(s, val, t, l, p)
    home(lambda s, r: lam.at[s, 0, :, r], lamh, 0, lambda s: s > 0)
    apply(a2, rest, True)

    while near and len(told) < rounds_for(groups):
        pass_on()
    heard(len(told) - 1)

    def gradient(s, total):
        for t, l, p in every():
            grad = lam[s, t, l, band(p)] - a2[s, t, l, padded(p)]
            grad += jnp.where(lev[s, t, band(p)] == float(l), omt[s, t, band(p)], 0.0)
            gg[s, t, l, band(p)] = grad
            a3[s, t, l, padded(p)] = grad
            if t == 0:
                total += grad * grad
        return total

    def prior_lam():
        @pl.when(first_group)
        def _():
            arrived(prior.at[0], rsem.at[1])
            arrived(bhal, rsem.at[2])

        @pl.when(jnp.logical_not(first_group))
        def _():
            arrived(prior.at[0], rsem.at[5])
            arrived(bhal, rsem.at[16])

        widen(prior, bhal)
        for t, l, p in every():
            lam[0, t, l, band(p)] = 0.5 * (x[0, t, l, band(p)] - prior[t, l, band(p)])

    def send_first():
        @pl.when(jnp.logical_not(first_group))
        def _():
            remote(gg.at[0, 0], gnext.at[0], 4, rsem.at[6], prv).start()
            squeeze(gsend, lambda l, p: gg[0, 1, l, band(p)])
            remote(gsend, ghal, 4, rsem.at[17], prv).start()

    def send_last():
        @pl.when(jnp.logical_not(last_group))
        def _():
            remote(
                a3.at[last, 0, :, pl.ds(rows, height)], prior2, 5, rsem.at[7], nxt
            ).start()

    total = jnp.zeros((rows, TILE), F32)
    if last > 0:
        prior_lam()
        total = gradient(0, total)
        send_first()
    @pl.when(jnp.logical_not(last_group))
    def _():
        arrived(x.at[per_group, 0], rsem.at[3])
        arrived(hnext, rsem.at[4])
        widen(x.at[per_group], hnext)

    has_later = jnp.where(last_group, 0.0, 1.0).astype(F32)
    for t, l, p in every():
        val = (0.5 * has_later) * (x[per_group, t, l, band(p)] - a1[last, t, l, padded(p)])
        first_adjoint(last, val, t, l, p)
    later_apply(a2)

    if last == 0:
        prior_lam()
    for s in range(1 if last > 0 else 0, per_group):
        total = gradient(s, total)
    if last == 0:
        send_first()
    row1[...] = jnp.sum(total, axis=0, keepdims=True)
    share(row1, slots1, 0)
    apply(a3, [last], False)
    send_last()
    home(lambda s, r: lam.at[s, 0, :, r], lamh, 0, lambda s: s == 0)
    home(lambda s, r: gg.at[s, 0, :, r], g1h, 1)
    apply(a3, rest, False)

    for s in rest:
        for t, l, p in every():
            q = gg[s + 1, t, l, band(p)] - a3[s, t, l, padded(p)]
            a4[s, t, l, padded(p)] = q
            if t == 0:
                qm[s + 1, l, band(p)] = q
    home(lambda s, r: qm.at[s, :, r], qh, 2, lambda s: s > 0)

    apply(a5, rest, True)
    later_apply(a5)
    for s in range(per_group):
        for p in range(bands):
            for l in range(levels):
                plain = (2.0 - 0.5 * variance[l]) * lam[s, 0, l, band(p)] - a5[s, 0, l, padded(p)]
                at_level = lev[s, 0, band(p)] == float(l)
                first[s, l, band(p)] = plain + jnp.where(at_level, 1.5 * omt[s, 0, band(p)], 0.0)

    apply(a4, rest, True)

    @pl.when(jnp.logical_not(last_group))
    def _():
        arrived(gnext.at[0], rsem.at[6])
        arrived(ghal, rsem.at[17])
        widen(gnext, ghal)

    for t, l, p in every():
        q = gnext[t, l, band(p)] - a3[last, t, l, padded(p)]
        a4[last, t, l, padded(p)] = has_later * q
    later_apply(a4)

    @pl.when(jnp.logical_not(first_group))
    def _():
        arrived(prior2, rsem.at[7])

    for _, l, p in every((0,)):
        qm[0, l, band(p)] = gg[0, 0, l, band(p)] - prior2[l, band(p)]
    home(lambda s, r: qm.at[s, :, r], qh, 2, lambda s: s == 0)


    for s in range(per_group):
        for p in range(bands):
            where = lev[s, 0, band(p)]
            seen = wgt[s, 0, band(p)] * pick(lambda l: gg[s, 0, l, band(p)], where)
            for l in range(levels):
                part = qm[s, l, band(p)] - a4[s, 0, l, padded(p)]
                second[s, l, band(p)] = part + jnp.where(where == float(l), seen, 0.0)

    c1 = gathered(row1, slots1, 0)
    h1 = 0.5 * c1

    total = jnp.zeros((rows, TILE), F32)
    for s in range(per_group):
        for l in range(levels):
            for p in range(bands):
                grad = first[s, l, band(p)] - h1 * second[s, l, band(p)]
                third[s, l, band(p)] = grad
                total += grad * grad
    row2[...] = jnp.sum(total, axis=0, keepdims=True)
    share(row2, slots2, 1)
    home(lambda s, r: third.at[s, :, r], g2, 3)

    arrived(g1h, rsem.at[9])
    for l in range(levels):
        xs[l] = xs[l] - c1 * g1h[l]
    for t in range(tiles):
        miss = pick(lambda l: xs[l, :, at(t)], levh[:, at(t)]) - raw[3, :, at(t)]
        om[:, at(t)] += 0.5 * (wgth[:, at(t)] * miss - om[:, at(t)])
    arrived(lamh, rsem.at[8])
    arrived(qh, rsem.at[10])
    for l in range(levels):
        m1[l] = (2.0 - 0.5 * variance[l]) * lamh[l] - h1 * qh[l]

    drain(ssem.at[0], (peers - 1) * (levels + 4 + nq + nl))
    for k in range(4):
        drain(ssem.at[6 + k], (peers - 1) * levels)

    @pl.when(first_group)
    def _():
        if bands > 1:
            drain(ssem.at[1], (bands - 1) * (levels + xq))

    @pl.when(jnp.logical_not(first_group))
    def _():
        drain(ssem.at[2], bands * (levels + xq))
        drain(ssem.at[4], bands * (levels + xq))

    @pl.when(jnp.logical_not(last_group))
    def _():
        drain(ssem.at[3], bands * (levels + xq))
        drain(ssem.at[5], bands * levels)

    arrived(g2, rsem.at[11])
    arrived(slots1, ssem.at[11])
    arrived(slots2, ssem.at[12])
    scale_out[...] = jnp.broadcast_to(gathered(row2, slots2, 1), (1, TILE))


def finish(x, mult, om, grad, scale, state_out, mult_out, om_out, state, sem):
    copies = [
        pltpu.make_async_copy(mult, mult_out.at[0], sem.at[0]),
        pltpu.make_async_copy(om, om_out.at[0], sem.at[1]),
    ]
    for c in copies:
        c.start()
    s = scale[0:1, 0:1]
    for l in range(x.shape[0]):
        state[l] = x[l] - s * grad[l]
    copies.append(pltpu.make_async_copy(state, state_out.at[0], sem.at[2]))
    copies[2].start()
    for c in copies:
        c.wait()


def on_device(subs, bands, *args):
    x = args[0]
    _, levels, rows, cols = x.shape
    n = subs * bands
    tiles = cols // TILE
    per_group = tiles // bands
    if per_group * bands != tiles or subs % per_group:
        raise ValueError("unsupported mesh")
    groups = subs // per_group
    height = bands * rows
    nq = -(-(levels + 3) // PER)
    nl = -(-4 // PER)
    xq = -(-levels // PER)
    dma = pltpu.SemaphoreType.DMA
    vm = lambda *shape: pltpu.VMEM(shape, F32)
    full = vm(levels, rows, cols)
    cell = vm(rows, cols)
    small = pltpu.VMEM((rows, tiles), jnp.int32)
    anywhere = pl.BlockSpec(memory_space=pltpu.HBM)
    vmem = pl.BlockSpec(memory_space=pltpu.VMEM)
    wide = vm(per_group, 2, levels, height + 2 * rows, TILE)
    pair = vm(2, levels, height, TILE)
    held = pl.pallas_call(
        functools.partial(kernel, subs, bands, per_group),
        out_shape=(full, full, cell, full, vm(1, TILE)),
        in_specs=[anywhere] * 10,
        out_specs=(vmem,) * 5,
        scratch_shapes=[
            vm(4, rows, cols),
            pltpu.SMEM((levels, levels), F32),
            pltpu.SMEM((levels,), F32),
            small,
            small,
            cell,
            cell,
            full,
            full,
            full,
            vm(tiles, nq, rows, TILE),
            vm(tiles, nl, rows, TILE),
            vm(per_group, bands, nq, rows, TILE),
            vm(per_group, bands, nl, rows, TILE),
            vm(bands, xq, rows, TILE),
            vm(4, per_group, height, TILE),
            vm(per_group + 1, 2, levels, height, TILE),
            vm(per_group + 1, 2, levels, height, TILE),
            vm(per_group, levels, height, TILE),
            vm(per_group, 2, levels, height, TILE),
            vm(per_group, levels, height, TILE),
            vm(per_group, levels, height, TILE),
            vm(per_group, levels, height, TILE),
            wide,
            wide,
            wide,
            wide,
            wide,
            wide,
            vm(per_group, 2, height + 2 * rows, TILE),
            vm(levels, per_group, 2, height, TILE),
            vm(5, per_group, 2, height, TILE),
            vm(per_group, 2, height, TILE),
            vm(per_group, 2, height, TILE),
            vm(per_group, 2, height, TILE),
            pair,
            vm(levels, height, TILE),
            pair,
            full,
            vm(bands, xq, rows, TILE),
            vm(bands, xq, rows, TILE),
            vm(bands, xq, rows, TILE),
            vm(bands, xq, rows, TILE),
            vm(bands, xq, rows, TILE),
            vm(1, TILE),
            vm(1, TILE),
            vm(n - 1, 1, TILE),
            vm(n - 1, 1, TILE),
            vm((tiles - 1) * (levels + 4 + nq + nl), rows, TILE),
            dma((10,)),
            dma((13,)),
            dma((19,)),
            dma((per_group,)),
            dma((per_group,)),
            pltpu.SemaphoreType.REGULAR((rounds_for(groups),)),
        ],
        compiler_params=pltpu.CompilerParams(
            collective_id=0,
            has_side_effects=True,
        ),
    )(*args)
    return pl.pallas_call(
        finish,
        out_shape=(
            jax.ShapeDtypeStruct(x.shape, F32),
            jax.ShapeDtypeStruct(x.shape, F32),
            jax.ShapeDtypeStruct((1, rows, cols), F32),
        ),
        in_specs=[vmem] * 5,
        out_specs=(anywhere,) * 3,
        scratch_shapes=[full, dma((3,))],
        compiler_params=pltpu.CompilerParams(vmem_limit_bytes=16 << 20),
    )(*held)


def solution(mesh):
    placed = (
        P("tm", None, "lat", None),
        P(None, "lat", None),
        P("tm", "lat", None),
        P("tm", "lat", None),
        P("tm", "lat", None),
        P("tm", "lat", None),
        P(),
        P(),
        P("tm", "lat", None),
        P("tm", "lat", None),
    )
    return jax.shard_map(
        functools.partial(on_device, mesh.shape["tm"], mesh.shape["lat"]),
        mesh=mesh,
        in_specs=placed,
        out_specs=(P("tm", None, "lat", None), P("tm", None, "lat", None), P("tm", "lat", None)),
        check_vma=False,
    )
```

```python
import functools

import jax
import jax.numpy as jnp
from jax import lax
from jax.experimental import pallas as pl
from jax.experimental.pallas import tpu as pltpu
from jax.sharding import PartitionSpec as P

TILE = 128
STEPS = 4
HALO = 4 * STEPS
SLOT = 2 * HALO
PER = TILE // SLOT
F32 = jnp.float32
MESH = pl.DeviceIdType.MESH


def offsets_for(groups):
    found, step = [], 1
    while step < groups:
        found.append(step)
        step *= 4
    return found


def rounds_for(groups):
    offsets, most = offsets_for(groups), 1
    for g in range(groups):
        dist, edge = {g: 0}, [g]
        for at in edge:
            for d in offsets:
                for t in (at - d, at + d):
                    if 0 <= t < groups and t not in dist:
                        dist[t] = dist[at] + 1
                        edge.append(t)
        most = max(most, max(dist.values()))
    return most


def kernel(
    subs,
    bands,
    per_group,
    x_hbm,
    bg_hbm,
    obs_hbm,
    kx_hbm,
    ky_hbm,
    ux_hbm,
    mix_hbm,
    var_hbm,
    lev_hbm,
    cls_hbm,
    xs,
    m1,
    om,
    g2,
    scale_out,
    raw,
    coupling,
    variance,
    lev_in,
    cls_in,
    levh,
    wgth,
    lamh,
    g1h,
    qh,
    packs,
    late,
    hal,
    hlate,
    hnext,
    main,
    x,
    lam,
    qm,
    gg,
    first,
    second,
    third,
    a1,
    a2,
    a3,
    a4,
    a5,
    bb,
    kyp,
    centre,
    coef,
    omt,
    wgt,
    lev,
    prior,
    prior2,
    gnext,
    bgv,
    bsrc,
    bhal,
    ghal,
    psend,
    gsend,
    row1,
    row2,
    slots1,
    slots2,
    spare,
    load_sem,
    ssem,
    rsem,
    rx,
    rh,
    gsem,
):
    j = lax.axis_index("tm")
    b = lax.axis_index("lat")
    n = subs * bands
    gme = j * bands + b
    levels, rows, cols = xs.shape
    tiles = cols // TILE
    height = bands * rows
    groups = subs // per_group
    peers = per_group * bands
    grp = j // per_group
    sme = lax.rem(j, per_group)
    me = sme * bands + b
    nq = hal.shape[2]
    nl = hlate.shape[2]
    xq = hnext.shape[1]
    first_group, last_group = grp == 0, grp == groups - 1
    last = per_group - 1

    def remote(src, dst, ss, rs, dev):
        return pltpu.make_async_remote_copy(
            src_ref=src,
            dst_ref=dst,
            send_sem=ssem.at[ss],
            recv_sem=rs,
            device_id=dev,
            device_id_type=MESH,
        )

    def peer(o):
        d = lax.rem(me + o, peers)
        return d, d // bands, lax.rem(d, bands), {
            "tm": grp * per_group + d // bands,
            "lat": lax.rem(d, bands),
        }

    def drain(sem, count):
        part = spare.at[0:count]
        pltpu.make_async_copy(part, part, sem).wait()

    def arrived(ref, sem):
        pltpu.make_async_copy(ref, ref, sem).wait()

    def lanes(t):
        return pl.ds(pl.multiple_of(t * TILE, TILE), TILE)

    def band(p):
        return pl.ds(rows * p, rows)

    def padded(p, shift=0):
        return pl.ds(rows + rows * p + shift, rows)

    def zero(ref):
        ref[...] = jnp.zeros(ref.shape, F32)

    nxt = {"tm": lax.rem(j + per_group, subs)}
    prv = {"tm": lax.rem(j + subs - per_group, subs)}
    barrier = pltpu.get_barrier_semaphore()

    near = []
    for d in offsets_for(groups):
        near += [(grp >= d, j - d * per_group), (grp + d < groups, j + d * per_group)]
    greeted = sum(jnp.where(ok, 1, 0) for ok, _ in near) if near else 0

    def greet(sem):
        for ok, t in near:
            @pl.when(ok)
            def _():
                pl.semaphore_signal(sem, inc=1, device_id={"tm": t}, device_id_type=MESH)

    for o in range(1, peers):
        pl.semaphore_signal(barrier, inc=1, device_id=peer(o)[3], device_id_type=MESH)
    greet(barrier)

    loads = [
        pltpu.make_async_copy(s, d, load_sem.at[i])
        for i, (s, d) in enumerate(
            [
                (x_hbm.at[0], xs),
                (kx_hbm.at[0], raw.at[0]),
                (ky_hbm.at[0], raw.at[1]),
                (ux_hbm.at[0], raw.at[2]),
                (obs_hbm.at[0], raw.at[3]),
                (lev_hbm.at[0], lev_in),
                (cls_hbm.at[0], cls_in),
                (mix_hbm, coupling),
                (var_hbm, variance),
            ]
        )
    ]
    for c in loads:
        c.start()
    load_bg = pltpu.make_async_copy(bg_hbm, bgv, load_sem.at[9])

    @pl.when(first_group)
    def _():
        load_bg.start()

    def zero_edges(ref):
        edge = jnp.zeros(ref.shape[:-2] + (rows, TILE), F32)
        ref[(slice(None),) * (len(ref.shape) - 2) + (pl.ds(0, rows),)] = edge
        ref[(slice(None),) * (len(ref.shape) - 2) + (pl.ds(rows + height, rows),)] = edge

    for ref in (a1, bb, kyp):
        zero_edges(ref)

    pl.semaphore_wait(barrier, peers - 1 + greeted)

    told = []

    def tell():
        if near and len(told) < rounds_for(groups):
            greet(gsem.at[len(told)])
            told.append(False)

    def heard(upto):
        for r in range(upto + 1):
            if not told[r]:
                pl.semaphore_wait(gsem.at[r], greeted)
                told[r] = True

    def pass_on():
        heard(len(told) - 1)
        tell()

    tell()

    own = lanes(me)
    fields = (kx_hbm, ky_hbm, ux_hbm)
    pltpu.make_async_copy(
        x_hbm.at[0, :, :, own], x.at[sme, 0, :, band(b)], rx.at[sme]
    ).start()
    for o in range(1, peers):
        d, _, _, dev = peer(o)
        remote(x_hbm.at[0, :, :, lanes(d)], x.at[sme, 0, :, band(b)], 0, rx.at[sme], dev).start()
    for i, f in enumerate(fields):
        pltpu.make_async_copy(f.at[0, :, own], main.at[i, sme, band(b)], rsem.at[0]).start()
    for o in range(1, peers):
        d, _, _, dev = peer(o)
        for i, f in enumerate(fields):
            remote(f.at[0, :, lanes(d)], main.at[i, sme, band(b)], 0, rsem.at[0], dev).start()

    lane = lax.broadcasted_iota(jnp.int32, (rows, TILE), 1)
    lane_first, lane_last = lane == 0, lane == TILE - 1
    right_side = lane < HALO
    inside = jnp.logical_or(right_side, lane >= TILE - HALO)
    place = lax.rem(lane + HALO, TILE) // SLOT

    def join(parts):
        out = parts[0]
        for k in range(1, len(parts)):
            out = jnp.where(place == k, parts[k], out)
        return out

    def turn(a, k):
        return a if k == 0 else pltpu.roll(a, SLOT * k, 1)

    def at(t):
        t = t % tiles
        return slice(t * TILE, (t + 1) * TILE)

    for c in loads:
        c.wait()

    for t in range(tiles):
        lev_t = jnp.broadcast_to(lev_in[:, t : t + 1], (rows, TILE))
        k = jnp.broadcast_to(cls_in[:, t : t + 1], (rows, TILE))
        levh[:, at(t)] = lev_t.astype(F32)
        wgth[:, at(t)] = jnp.where(
            k == 0, 1.0, jnp.where(k == 1, 0.5, jnp.where(k == 2, 0.25, 0.0))
        ).astype(F32)

    def field(f, t):
        if f < levels:
            return xs[f, :, at(t)]
        if f < levels + 4:
            return raw[f - levels, :, at(t)]
        return (wgth if f == levels + 4 else levh)[:, at(t)]

    def pack(dst, q, held, extra=None):
        moved = [[turn(field(f, t), i) for i, f in enumerate(held)] for t in range(tiles)]
        for d in range(tiles):
            parts = []
            for i in range(len(held)):
                side = jnp.logical_and(lane >= SLOT * i, lane < SLOT * i + HALO)
                parts.append(
                    jnp.where(side, moved[(d + 1) % tiles][i], moved[(d - 1) % tiles][i])
                )
            if extra is not None:
                parts.append(extra(d))
            dst[d, q] = join(parts)

    early = levels + 3
    for q in range(nq):
        pack(packs, q, range(q * PER, min((q + 1) * PER, early)))
    for o in range(1, peers):
        d, _, _, dev = peer(o)
        remote(packs.at[d], hal.at[sme, b], 0, rh.at[sme], dev).start()
    pltpu.make_async_copy(packs.at[me], hal.at[sme, b], rh.at[sme]).start()

    front = lax.rem(lane + HALO, SLOT) < HALO
    pack(
        late,
        0,
        range(early, early + 3),
        lambda d: jnp.where(front, wgth[:, at(d)], levh[:, at(d)]),
    )
    pltpu.make_async_copy(obs_hbm.at[0, :, own], main.at[3, sme, band(b)], rsem.at[15]).start()
    pltpu.make_async_copy(late.at[me], hlate.at[sme, b], rsem.at[18]).start()
    for o in range(1, peers):
        d, _, _, dev = peer(o)
        remote(obs_hbm.at[0, :, lanes(d)], main.at[3, sme, band(b)], 0, rsem.at[15], dev).start()
        remote(late.at[d], hlate.at[sme, b], 0, rsem.at[18], dev).start()

    pass_on()

    @pl.when(first_group)
    def _():
        load_bg.wait()
        for o in range(bands):
            e = lax.rem(b + o, bands)
            d = sme * bands + e
            lo, hi = lanes(lax.rem(d + tiles - 1, tiles)), lanes(lax.rem(d + 1, tiles))
            for q in range(xq):
                bsrc[o, q] = join(
                    [
                        turn(jnp.where(right_side, bgv[l, :, hi], bgv[l, :, lo]), l - q * PER)
                        for l in range(q * PER, min((q + 1) * PER, levels))
                    ]
                )
            src = bg_hbm.at[:, :, lanes(d)]
            if o == 0:
                pltpu.make_async_copy(src, prior.at[0, :, band(b)], rsem.at[1]).start()
                pltpu.make_async_copy(bsrc.at[0], bhal.at[b], rsem.at[2]).start()
            else:
                remote(src, prior.at[0, :, band(b)], 1, rsem.at[1], {"lat": e}).start()
                remote(bsrc.at[o], bhal.at[b], 1, rsem.at[2], {"lat": e}).start()
        zero(prior2)

    @pl.when(last_group)
    def _():
        zero(x.at[per_group])
        zero(gnext)

    def pick(get, choice):
        out = jnp.where(choice == 0.0, get(0), 0.0)
        for l in range(1, levels):
            out += jnp.where(choice == float(l), get(l), 0.0)
        return out

    for t in range(tiles):
        miss = pick(lambda l: xs[l, :, at(t)], levh[:, at(t)]) - raw[3, :, at(t)]
        om[:, at(t)] = 0.5 * (wgth[:, at(t)] * miss)

    arrived(x.at[0, 0], rx.at[0])

    @pl.when(jnp.logical_not(first_group))
    def _():
        remote(x.at[0, 0], x.at[per_group, 0], 2, rsem.at[3], prv).start()

    arrived(hal.at[0], rh.at[0])

    @pl.when(jnp.logical_not(first_group))
    def _():
        remote(hal.at[0, :, 0:xq], hnext, 2, rsem.at[4], prv).start()

    pass_on()

    for s in range(1, per_group):
        arrived(x.at[s, 0], rx.at[s])
        arrived(hal.at[s], rh.at[s])
    arrived(main.at[0:3], rsem.at[0])

    def unpack(ref, f):
        return jnp.where(inside, turn(ref[f // PER], (PER - f % PER) % PER), 0.0)

    def column(a, c):
        return jnp.broadcast_to(a[:, c : c + 1], (rows, TILE))

    mix = [[coupling[l, m] for m in range(levels)] for l in range(levels)]

    def prepare(s):
        for p in range(bands):
            got = hal.at[s, p]
            for l in range(levels):
                a1[s, 0, l, padded(p)] = x[s, 0, l, band(p)]
                val = unpack(got, l)
                x[s, 1, l, band(p)] = val
                a1[s, 1, l, padded(p)] = val
            for t in range(2):
                kx, ky, ux = (
                    main[i, s, band(p)] if t == 0 else unpack(got, levels + i) for i in range(3)
                )
                plain = 1.0 - 2.0 * kx - 2.0 * ky
                for l in range(levels):
                    centre[l, s, t, band(p)] = plain + mix[l][l]
                coef[1, s, t, band(p)] = kx + 0.5 * ux
                coef[2, s, t, band(p)] = kx - 0.5 * ux
                kyp[s, t, padded(p)] = ky

    def prepare_late(s):
        for p in range(bands):
            for t in range(2):
                coef[3, s, t, band(p)] = east(*(coef[2, s, k, band(p)] for k in (t, 1 - t)))
                coef[4, s, t, band(p)] = west(*(coef[1, s, k, band(p)] for k in (t, 1 - t)))
            got = hlate.at[s, p]
            wgt[s, 1, band(p)] = unpack(got, 1)
            lev[s, 1, band(p)] = unpack(got, 2)
            info = got[3 // PER]
            base = SLOT * (3 % PER)
            wgt[s, 0, band(p)] = column(info, (base + TILE - HALO) % TILE)
            lev[s, 0, band(p)] = column(info, base)
            for t in range(2):
                ob = main[3, s, band(p)] if t == 0 else unpack(got, 0)
                miss = pick(lambda l: x[s, t, l, band(p)], lev[s, t, band(p)]) - ob
                omt[s, t, band(p)] = 0.5 * (wgt[s, t, band(p)] * miss)

    def east(a, after):
        return pltpu.roll(jnp.where(lane_first, after, a), TILE - 1, 1)

    def west(a, before):
        return pltpu.roll(jnp.where(lane_last, before, a), 1, 1)

    def step(src, dst, s, p, adjoint):
        v = [[src[s, t, l, padded(p)] for l in range(levels)] for t in range(2)]
        for t in range(2):
            ce, cw = (coef[k + 2 * adjoint, s, t, band(p)] for k in (1, 2))
            if adjoint:
                cu, cd = kyp[s, t, padded(p, 1)], kyp[s, t, padded(p, -1)]
            else:
                cr = kyp[s, t, padded(p)]
            for l in range(levels):
                a, o = v[t][l], v[1 - t][l]
                up, down = src[s, t, l, padded(p, 1)], src[s, t, l, padded(p, -1)]
                out = centre[l, s, t, band(p)] * a
                for m in range(levels):
                    if m != l:
                        out += (mix[m][l] if adjoint else mix[l][m]) * v[t][m]
                if adjoint:
                    out += cu * up
                    out += cd * down
                else:
                    out += cr * (up + down)
                out += ce * east(a, o)
                out += cw * west(a, o)
                dst[s, t, l, padded(p)] = out

    def apply(buf, which, adjoint):
        if not which:
            return

        def body(_, carry):
            for src, dst in ((buf, bb), (bb, buf)):
                for s in which:
                    for p in range(bands):
                        step(src, dst, s, p, adjoint)
            return carry

        if len(which) == 1:
            for k in range(STEPS // 2):
                body(k, 0)
        else:
            lax.fori_loop(0, STEPS // 2, body, 0)

    def every(which=(0, 1)):
        return [(t, l, p) for t in which for l in range(levels) for p in range(bands)]

    def squeeze(dst, get):
        for p in range(bands):
            for q in range(xq):
                dst[p, q] = join(
                    [turn(get(l, p), l - q * PER) for l in range(q * PER, min((q + 1) * PER, levels))]
                )

    def widen(dst, src):
        for l in range(levels):
            for p in range(bands):
                dst[1, l, band(p)] = unpack(src.at[p], l)

    def home(src, dst, k, wanted=None):
        for o in range(1, peers):
            _, s, p, dev = peer(o)

            def send():
                remote(
                    src(s, pl.ds(pl.multiple_of(p * rows, rows), rows)),
                    dst.at[:, :, own],
                    6 + k,
                    rsem.at[8 + k],
                    dev,
                ).start()

            if wanted is None:
                send()
            else:
                pl.when(wanted(s))(send)

        def keep():
            mine = src(sme, pl.ds(pl.multiple_of(b * rows, rows), rows))
            pltpu.make_async_copy(mine, dst.at[:, :, own], rsem.at[8 + k]).start()

        if wanted is None:
            keep()
        else:
            pl.when(wanted(sme))(keep)

    def share(src, slots, k):
        def body(t, carry):
            o = lax.rem(t + n - gme, n)

            @pl.when(o > 0)
            def _():
                dev = {"tm": t // bands, "lat": t % bands}
                remote(src, slots.at[o - 1], 11 + k, rsem.at[13 + k], dev).start()

            return carry

        if n > 64:
            lax.fori_loop(0, n, body, 0)
        else:
            for t in range(n):
                body(t, 0)

    def gathered(row, slots, k):
        arrived(slots, rsem.at[13 + k])
        full = jnp.sum(row[...] + jnp.sum(slots[...], axis=0), axis=1, keepdims=True)
        size = float(levels * rows * cols * n)
        return 0.3 / jnp.sqrt(full / size + 1e-6)

    rest = list(range(last))

    prepare(last)
    apply(a1, [last], False)

    @pl.when(jnp.logical_not(last_group))
    def _():
        remote(a1.at[last, 0, :, pl.ds(rows, height)], prior.at[0], 3, rsem.at[5], nxt).start()
        squeeze(psend, lambda l, p: a1[last, 1, l, padded(p)])
        remote(psend, bhal, 3, rsem.at[16], nxt).start()

    for s in rest:
        prepare(s)
    apply(a1, rest, False)

    arrived(main.at[3], rsem.at[15])
    arrived(hlate, rsem.at[18])
    for s in range(per_group):
        prepare_late(s)
    for ref in (a2, a3, a4, a5):
        zero_edges(ref)

    def later_apply(buf):
        @pl.when(jnp.logical_not(last_group))
        def _():
            apply(buf, [last], True)

    def first_adjoint(s, val, t, l, p):
        lam[s + 1, t, l, band(p)] = val
        a2[s, t, l, padded(p)] = val
        a5[s, t, l, padded(p)] = (2.0 - 0.5 * variance[l]) * val

    for s in rest:
        for t, l, p in every():
            val = 0.5 * (x[s + 1, t, l, band(p)] - a1[s, t, l, padded(p)])
            first_adjoint(s, val, t, l, p)
    home(lambda s, r: lam.at[s, 0, :, r], lamh, 0, lambda s: s > 0)
    apply(a2, rest, True)

    while near and len(told) < rounds_for(groups):
        pass_on()
    heard(len(told) - 1)

    def gradient(s, total):
        for t, l, p in every():
            grad = lam[s, t, l, band(p)] - a2[s, t, l, padded(p)]
            grad += jnp.where(lev[s, t, band(p)] == float(l), omt[s, t, band(p)], 0.0)
            gg[s, t, l, band(p)] = grad
            a3[s, t, l, padded(p)] = grad
            if t == 0:
                total += grad * grad
        return total

    def prior_lam():
        @pl.when(first_group)
        def _():
            arrived(prior.at[0], rsem.at[1])
            arrived(bhal, rsem.at[2])

        @pl.when(jnp.logical_not(first_group))
        def _():
            arrived(prior.at[0], rsem.at[5])
            arrived(bhal, rsem.at[16])

        widen(prior, bhal)
        for t, l, p in every():
            lam[0, t, l, band(p)] = 0.5 * (x[0, t, l, band(p)] - prior[t, l, band(p)])

    def send_first():
        @pl.when(jnp.logical_not(first_group))
        def _():
            remote(gg.at[0, 0], gnext.at[0], 4, rsem.at[6], prv).start()
            squeeze(gsend, lambda l, p: gg[0, 1, l, band(p)])
            remote(gsend, ghal, 4, rsem.at[17], prv).start()

    def send_last():
        @pl.when(jnp.logical_not(last_group))
        def _():
            remote(
                a3.at[last, 0, :, pl.ds(rows, height)], prior2, 5, rsem.at[7], nxt
            ).start()

    total = jnp.zeros((rows, TILE), F32)
    if last > 0:
        prior_lam()
        total = gradient(0, total)
        send_first()
    @pl.when(jnp.logical_not(last_group))
    def _():
        arrived(x.at[per_group, 0], rsem.at[3])
        arrived(hnext, rsem.at[4])
        widen(x.at[per_group], hnext)

    has_later = jnp.where(last_group, 0.0, 1.0).astype(F32)
    for t, l, p in every():
        val = (0.5 * has_later) * (x[per_group, t, l, band(p)] - a1[last, t, l, padded(p)])
        first_adjoint(last, val, t, l, p)
    later_apply(a2)

    if last == 0:
        prior_lam()
    for s in range(1 if last > 0 else 0, per_group):
        total = gradient(s, total)
    if last == 0:
        send_first()
    row1[...] = jnp.sum(total, axis=0, keepdims=True)
    share(row1, slots1, 0)
    apply(a3, [last], False)
    send_last()
    home(lambda s, r: lam.at[s, 0, :, r], lamh, 0, lambda s: s == 0)
    home(lambda s, r: gg.at[s, 0, :, r], g1h, 1)
    apply(a3, rest, False)

    for s in rest:
        for t, l, p in every():
            q = gg[s + 1, t, l, band(p)] - a3[s, t, l, padded(p)]
            a4[s, t, l, padded(p)] = q
            if t == 0:
                qm[s + 1, l, band(p)] = q
    home(lambda s, r: qm.at[s, :, r], qh, 2, lambda s: s > 0)

    @pl.when(last_group)
    def _():
        apply(a5, rest, True)

    @pl.when(jnp.logical_not(last_group))
    def _():
        apply(a5, list(range(per_group)), True)

    for s in range(per_group):
        for p in range(bands):
            for l in range(levels):
                plain = (2.0 - 0.5 * variance[l]) * lam[s, 0, l, band(p)] - a5[s, 0, l, padded(p)]
                at_level = lev[s, 0, band(p)] == float(l)
                first[s, l, band(p)] = plain + jnp.where(at_level, 1.5 * omt[s, 0, band(p)], 0.0)

    apply(a4, rest, True)

    @pl.when(jnp.logical_not(last_group))
    def _():
        arrived(gnext.at[0], rsem.at[6])
        arrived(ghal, rsem.at[17])
        widen(gnext, ghal)

    for t, l, p in every():
        q = gnext[t, l, band(p)] - a3[last, t, l, padded(p)]
        a4[last, t, l, padded(p)] = has_later * q
    later_apply(a4)

    @pl.when(jnp.logical_not(first_group))
    def _():
        arrived(prior2, rsem.at[7])

    for _, l, p in every((0,)):
        qm[0, l, band(p)] = gg[0, 0, l, band(p)] - prior2[l, band(p)]
    home(lambda s, r: qm.at[s, :, r], qh, 2, lambda s: s == 0)


    for s in range(per_group):
        for p in range(bands):
            where = lev[s, 0, band(p)]
            seen = wgt[s, 0, band(p)] * pick(lambda l: gg[s, 0, l, band(p)], where)
            for l in range(levels):
                part = qm[s, l, band(p)] - a4[s, 0, l, padded(p)]
                second[s, l, band(p)] = part + jnp.where(where == float(l), seen, 0.0)

    c1 = gathered(row1, slots1, 0)
    h1 = 0.5 * c1

    total = jnp.zeros((rows, TILE), F32)
    for s in range(per_group):
        for l in range(levels):
            for p in range(bands):
                grad = first[s, l, band(p)] - h1 * second[s, l, band(p)]
                third[s, l, band(p)] = grad
                total += grad * grad
    row2[...] = jnp.sum(total, axis=0, keepdims=True)
    share(row2, slots2, 1)
    home(lambda s, r: third.at[s, :, r], g2, 3)

    arrived(g1h, rsem.at[9])
    for l in range(levels):
        xs[l] = xs[l] - c1 * g1h[l]
    for t in range(tiles):
        miss = pick(lambda l: xs[l, :, at(t)], levh[:, at(t)]) - raw[3, :, at(t)]
        om[:, at(t)] += 0.5 * (wgth[:, at(t)] * miss - om[:, at(t)])
    arrived(lamh, rsem.at[8])
    arrived(qh, rsem.at[10])
    for l in range(levels):
        m1[l] = (2.0 - 0.5 * variance[l]) * lamh[l] - h1 * qh[l]

    drain(ssem.at[0], (peers - 1) * (levels + 4 + nq + nl))
    for k in range(4):
        drain(ssem.at[6 + k], (peers - 1) * levels)

    @pl.when(first_group)
    def _():
        if bands > 1:
            drain(ssem.at[1], (bands - 1) * (levels + xq))

    @pl.when(jnp.logical_not(first_group))
    def _():
        drain(ssem.at[2], bands * (levels + xq))
        drain(ssem.at[4], bands * (levels + xq))

    @pl.when(jnp.logical_not(last_group))
    def _():
        drain(ssem.at[3], bands * (levels + xq))
        drain(ssem.at[5], bands * levels)

    arrived(g2, rsem.at[11])
    arrived(slots1, ssem.at[11])
    arrived(slots2, ssem.at[12])
    scale_out[...] = jnp.broadcast_to(gathered(row2, slots2, 1), (1, TILE))


def finish(x, mult, om, grad, scale, state_out, mult_out, om_out, state, sem):
    copies = [
        pltpu.make_async_copy(mult, mult_out.at[0], sem.at[0]),
        pltpu.make_async_copy(om, om_out.at[0], sem.at[1]),
    ]
    for c in copies:
        c.start()
    s = scale[0:1, 0:1]
    for l in range(x.shape[0]):
        state[l] = x[l] - s * grad[l]
    copies.append(pltpu.make_async_copy(state, state_out.at[0], sem.at[2]))
    copies[2].start()
    for c in copies:
        c.wait()


def on_device(subs, bands, *args):
    x = args[0]
    _, levels, rows, cols = x.shape
    n = subs * bands
    tiles = cols // TILE
    per_group = tiles // bands
    if per_group * bands != tiles or subs % per_group:
        raise ValueError("unsupported mesh")
    groups = subs // per_group
    height = bands * rows
    nq = -(-(levels + 3) // PER)
    nl = -(-4 // PER)
    xq = -(-levels // PER)
    dma = pltpu.SemaphoreType.DMA
    vm = lambda *shape: pltpu.VMEM(shape, F32)
    full = vm(levels, rows, cols)
    cell = vm(rows, cols)
    small = pltpu.VMEM((rows, tiles), jnp.int32)
    anywhere = pl.BlockSpec(memory_space=pltpu.HBM)
    vmem = pl.BlockSpec(memory_space=pltpu.VMEM)
    wide = vm(per_group, 2, levels, height + 2 * rows, TILE)
    pair = vm(2, levels, height, TILE)
    held = pl.pallas_call(
        functools.partial(kernel, subs, bands, per_group),
        out_shape=(full, full, cell, full, vm(1, TILE)),
        in_specs=[anywhere] * 10,
        out_specs=(vmem,) * 5,
        scratch_shapes=[
            vm(4, rows, cols),
            pltpu.SMEM((levels, levels), F32),
            pltpu.SMEM((levels,), F32),
            small,
            small,
            cell,
            cell,
            full,
            full,
            full,
            vm(tiles, nq, rows, TILE),
            vm(tiles, nl, rows, TILE),
            vm(per_group, bands, nq, rows, TILE),
            vm(per_group, bands, nl, rows, TILE),
            vm(bands, xq, rows, TILE),
            vm(4, per_group, height, TILE),
            vm(per_group + 1, 2, levels, height, TILE),
            vm(per_group + 1, 2, levels, height, TILE),
            vm(per_group, levels, height, TILE),
            vm(per_group, 2, levels, height, TILE),
            vm(per_group, levels, height, TILE),
            vm(per_group, levels, height, TILE),
            vm(per_group, levels, height, TILE),
            wide,
            wide,
            wide,
            wide,
            wide,
            wide,
            vm(per_group, 2, height + 2 * rows, TILE),
            vm(levels, per_group, 2, height, TILE),
            vm(5, per_group, 2, height, TILE),
            vm(per_group, 2, height, TILE),
            vm(per_group, 2, height, TILE),
            vm(per_group, 2, height, TILE),
            pair,
            vm(levels, height, TILE),
            pair,
            full,
            vm(bands, xq, rows, TILE),
            vm(bands, xq, rows, TILE),
            vm(bands, xq, rows, TILE),
            vm(bands, xq, rows, TILE),
            vm(bands, xq, rows, TILE),
            vm(1, TILE),
            vm(1, TILE),
            vm(n - 1, 1, TILE),
            vm(n - 1, 1, TILE),
            vm((tiles - 1) * (levels + 4 + nq + nl), rows, TILE),
            dma((10,)),
            dma((13,)),
            dma((19,)),
            dma((per_group,)),
            dma((per_group,)),
            pltpu.SemaphoreType.REGULAR((rounds_for(groups),)),
        ],
        compiler_params=pltpu.CompilerParams(
            collective_id=0,
            has_side_effects=True,
        ),
    )(*args)
    return pl.pallas_call(
        finish,
        out_shape=(
            jax.ShapeDtypeStruct(x.shape, F32),
            jax.ShapeDtypeStruct(x.shape, F32),
            jax.ShapeDtypeStruct((1, rows, cols), F32),
        ),
        in_specs=[vmem] * 5,
        out_specs=(anywhere,) * 3,
        scratch_shapes=[full, dma((3,))],
        compiler_params=pltpu.CompilerParams(vmem_limit_bytes=16 << 20),
    )(*held)


def solution(mesh):
    placed = (
        P("tm", None, "lat", None),
        P(None, "lat", None),
        P("tm", "lat", None),
        P("tm", "lat", None),
        P("tm", "lat", None),
        P("tm", "lat", None),
        P(),
        P(),
        P("tm", "lat", None),
        P("tm", "lat", None),
    )
    return jax.shard_map(
        functools.partial(on_device, mesh.shape["tm"], mesh.shape["lat"]),
        mesh=mesh,
        in_specs=placed,
        out_specs=(P("tm", None, "lat", None), P("tm", None, "lat", None), P("tm", "lat", None)),
        check_vma=False,
    )
```

```python
import functools

import jax
import jax.numpy as jnp
from jax import lax
from jax.experimental import pallas as pl
from jax.experimental.pallas import tpu as pltpu
from jax.sharding import PartitionSpec as P

TILE = 128
STEPS = 4
HALO = 4 * STEPS
SLOT = 2 * HALO
PER = TILE // SLOT
F32 = jnp.float32
MESH = pl.DeviceIdType.MESH


def offsets_for(groups):
    found, step = [], 1
    while step < groups:
        found.append(step)
        step *= 4
    return found


def rounds_for(groups):
    offsets, most = offsets_for(groups), 1
    for g in range(groups):
        dist, edge = {g: 0}, [g]
        for at in edge:
            for d in offsets:
                for t in (at - d, at + d):
                    if 0 <= t < groups and t not in dist:
                        dist[t] = dist[at] + 1
                        edge.append(t)
        most = max(most, max(dist.values()))
    return most


def kernel(
    subs,
    bands,
    per_group,
    x_hbm,
    bg_hbm,
    obs_hbm,
    kx_hbm,
    ky_hbm,
    ux_hbm,
    mix_hbm,
    var_hbm,
    lev_hbm,
    cls_hbm,
    xs,
    m1,
    om,
    g2,
    scale_out,
    raw,
    coupling,
    variance,
    lev_in,
    cls_in,
    levh,
    wgth,
    lamh,
    g1h,
    qh,
    packs,
    late,
    hal,
    hlate,
    hnext,
    main,
    x,
    lam,
    qm,
    gg,
    first,
    second,
    third,
    a1,
    a2,
    a3,
    a4,
    a5,
    bb,
    kyp,
    centre,
    coef,
    omt,
    wgt,
    lev,
    prior,
    prior2,
    gnext,
    bgv,
    bsrc,
    bhal,
    ghal,
    psend,
    gsend,
    row1,
    row2,
    slots1,
    slots2,
    spare,
    load_sem,
    ssem,
    rsem,
    rx,
    rh,
    gsem,
):
    j = lax.axis_index("tm")
    b = lax.axis_index("lat")
    n = subs * bands
    gme = j * bands + b
    levels, rows, cols = xs.shape
    tiles = cols // TILE
    height = bands * rows
    groups = subs // per_group
    peers = per_group * bands
    grp = j // per_group
    sme = lax.rem(j, per_group)
    me = sme * bands + b
    nq = hal.shape[2]
    nl = hlate.shape[2]
    xq = hnext.shape[1]
    first_group, last_group = grp == 0, grp == groups - 1
    last = per_group - 1

    def remote(src, dst, ss, rs, dev):
        return pltpu.make_async_remote_copy(
            src_ref=src,
            dst_ref=dst,
            send_sem=ssem.at[ss],
            recv_sem=rs,
            device_id=dev,
            device_id_type=MESH,
        )

    def peer(o):
        d = lax.rem(me + o, peers)
        return d, d // bands, lax.rem(d, bands), {
            "tm": grp * per_group + d // bands,
            "lat": lax.rem(d, bands),
        }

    def drain(sem, count):
        part = spare.at[0:count]
        pltpu.make_async_copy(part, part, sem).wait()

    def arrived(ref, sem):
        pltpu.make_async_copy(ref, ref, sem).wait()

    def lanes(t):
        return pl.ds(pl.multiple_of(t * TILE, TILE), TILE)

    def band(p):
        return pl.ds(rows * p, rows)

    def padded(p, shift=0):
        return pl.ds(rows + rows * p + shift, rows)

    def zero(ref):
        ref[...] = jnp.zeros(ref.shape, F32)

    nxt = {"tm": lax.rem(j + per_group, subs)}
    prv = {"tm": lax.rem(j + subs - per_group, subs)}
    barrier = pltpu.get_barrier_semaphore()

    near = []
    for d in offsets_for(groups):
        near += [(grp >= d, j - d * per_group), (grp + d < groups, j + d * per_group)]
    greeted = sum(jnp.where(ok, 1, 0) for ok, _ in near) if near else 0

    def greet(sem):
        for ok, t in near:
            @pl.when(ok)
            def _():
                pl.semaphore_signal(sem, inc=1, device_id={"tm": t}, device_id_type=MESH)

    for o in range(1, peers):
        pl.semaphore_signal(barrier, inc=1, device_id=peer(o)[3], device_id_type=MESH)
    greet(barrier)

    loads = [
        pltpu.make_async_copy(s, d, load_sem.at[i])
        for i, (s, d) in enumerate(
            [
                (x_hbm.at[0], xs),
                (kx_hbm.at[0], raw.at[0]),
                (ky_hbm.at[0], raw.at[1]),
                (ux_hbm.at[0], raw.at[2]),
                (obs_hbm.at[0], raw.at[3]),
                (lev_hbm.at[0], lev_in),
                (cls_hbm.at[0], cls_in),
                (mix_hbm, coupling),
                (var_hbm, variance),
            ]
        )
    ]
    for c in loads:
        c.start()
    load_bg = pltpu.make_async_copy(bg_hbm, bgv, load_sem.at[9])

    @pl.when(first_group)
    def _():
        load_bg.start()

    def zero_edges(ref):
        edge = jnp.zeros(ref.shape[:-2] + (rows, TILE), F32)
        ref[(slice(None),) * (len(ref.shape) - 2) + (pl.ds(0, rows),)] = edge
        ref[(slice(None),) * (len(ref.shape) - 2) + (pl.ds(rows + height, rows),)] = edge

    for ref in (a1, bb, kyp):
        zero_edges(ref)

    pl.semaphore_wait(barrier, peers - 1 + greeted)

    told = []

    def tell():
        if near and len(told) < rounds_for(groups):
            greet(gsem.at[len(told)])
            told.append(False)

    def heard(upto):
        for r in range(upto + 1):
            if not told[r]:
                pl.semaphore_wait(gsem.at[r], greeted)
                told[r] = True

    def pass_on():
        heard(len(told) - 1)
        tell()

    tell()

    own = lanes(me)
    fields = (kx_hbm, ky_hbm, ux_hbm)
    pltpu.make_async_copy(
        x_hbm.at[0, :, :, own], x.at[sme, 0, :, band(b)], rx.at[sme]
    ).start()
    for o in range(1, peers):
        d, _, _, dev = peer(o)
        remote(x_hbm.at[0, :, :, lanes(d)], x.at[sme, 0, :, band(b)], 0, rx.at[sme], dev).start()
    for i, f in enumerate(fields):
        pltpu.make_async_copy(f.at[0, :, own], main.at[i, sme, band(b)], rsem.at[0]).start()
    for o in range(1, peers):
        d, _, _, dev = peer(o)
        for i, f in enumerate(fields):
            remote(f.at[0, :, lanes(d)], main.at[i, sme, band(b)], 0, rsem.at[0], dev).start()

    lane = lax.broadcasted_iota(jnp.int32, (rows, TILE), 1)
    lane_first, lane_last = lane == 0, lane == TILE - 1
    right_side = lane < HALO
    inside = jnp.logical_or(right_side, lane >= TILE - HALO)
    place = lax.rem(lane + HALO, TILE) // SLOT

    def join(parts):
        out = parts[0]
        for k in range(1, len(parts)):
            out = jnp.where(place == k, parts[k], out)
        return out

    def turn(a, k):
        return a if k == 0 else pltpu.roll(a, SLOT * k, 1)

    def at(t):
        t = t % tiles
        return slice(t * TILE, (t + 1) * TILE)

    for c in loads:
        c.wait()

    for t in range(tiles):
        lev_t = jnp.broadcast_to(lev_in[:, t : t + 1], (rows, TILE))
        k = jnp.broadcast_to(cls_in[:, t : t + 1], (rows, TILE))
        levh[:, at(t)] = lev_t.astype(F32)
        wgth[:, at(t)] = jnp.where(
            k == 0, 1.0, jnp.where(k == 1, 0.5, jnp.where(k == 2, 0.25, 0.0))
        ).astype(F32)

    def field(f, t):
        if f < levels:
            return xs[f, :, at(t)]
        if f < levels + 4:
            return raw[f - levels, :, at(t)]
        return (wgth if f == levels + 4 else levh)[:, at(t)]

    def pack(dst, q, held, extra=None):
        moved = [[turn(field(f, t), i) for i, f in enumerate(held)] for t in range(tiles)]
        for d in range(tiles):
            parts = []
            for i in range(len(held)):
                side = jnp.logical_and(lane >= SLOT * i, lane < SLOT * i + HALO)
                parts.append(
                    jnp.where(side, moved[(d + 1) % tiles][i], moved[(d - 1) % tiles][i])
                )
            if extra is not None:
                parts.append(extra(d))
            dst[d, q] = join(parts)

    early = levels + 3
    for q in range(nq):
        pack(packs, q, range(q * PER, min((q + 1) * PER, early)))
    for o in range(1, peers):
        d, _, _, dev = peer(o)
        remote(packs.at[d], hal.at[sme, b], 0, rh.at[sme], dev).start()
    pltpu.make_async_copy(packs.at[me], hal.at[sme, b], rh.at[sme]).start()

    front = lax.rem(lane + HALO, SLOT) < HALO
    pack(
        late,
        0,
        range(early, early + 3),
        lambda d: jnp.where(front, wgth[:, at(d)], levh[:, at(d)]),
    )
    pltpu.make_async_copy(obs_hbm.at[0, :, own], main.at[3, sme, band(b)], rsem.at[15]).start()
    pltpu.make_async_copy(late.at[me], hlate.at[sme, b], rsem.at[18]).start()
    for o in range(1, peers):
        d, _, _, dev = peer(o)
        remote(obs_hbm.at[0, :, lanes(d)], main.at[3, sme, band(b)], 0, rsem.at[15], dev).start()
        remote(late.at[d], hlate.at[sme, b], 0, rsem.at[18], dev).start()

    pass_on()

    @pl.when(first_group)
    def _():
        load_bg.wait()
        for o in range(bands):
            e = lax.rem(b + o, bands)
            d = sme * bands + e
            lo, hi = lanes(lax.rem(d + tiles - 1, tiles)), lanes(lax.rem(d + 1, tiles))
            for q in range(xq):
                bsrc[o, q] = join(
                    [
                        turn(jnp.where(right_side, bgv[l, :, hi], bgv[l, :, lo]), l - q * PER)
                        for l in range(q * PER, min((q + 1) * PER, levels))
                    ]
                )
            src = bg_hbm.at[:, :, lanes(d)]
            if o == 0:
                pltpu.make_async_copy(src, prior.at[0, :, band(b)], rsem.at[1]).start()
                pltpu.make_async_copy(bsrc.at[0], bhal.at[b], rsem.at[2]).start()
            else:
                remote(src, prior.at[0, :, band(b)], 1, rsem.at[1], {"lat": e}).start()
                remote(bsrc.at[o], bhal.at[b], 1, rsem.at[2], {"lat": e}).start()
        zero(prior2)

    @pl.when(last_group)
    def _():
        zero(x.at[per_group])
        zero(gnext)

    def pick(get, choice):
        out = jnp.where(choice == 0.0, get(0), 0.0)
        for l in range(1, levels):
            out += jnp.where(choice == float(l), get(l), 0.0)
        return out

    for t in range(tiles):
        miss = pick(lambda l: xs[l, :, at(t)], levh[:, at(t)]) - raw[3, :, at(t)]
        om[:, at(t)] = 0.5 * (wgth[:, at(t)] * miss)

    arrived(x.at[0, 0], rx.at[0])

    @pl.when(jnp.logical_not(first_group))
    def _():
        remote(x.at[0, 0], x.at[per_group, 0], 2, rsem.at[3], prv).start()

    arrived(hal.at[0], rh.at[0])

    @pl.when(jnp.logical_not(first_group))
    def _():
        remote(hal.at[0, :, 0:xq], hnext, 2, rsem.at[4], prv).start()

    pass_on()

    for s in range(1, per_group):
        arrived(x.at[s, 0], rx.at[s])
        arrived(hal.at[s], rh.at[s])
    arrived(main.at[0:3], rsem.at[0])

    def unpack(ref, f):
        return jnp.where(inside, turn(ref[f // PER], (PER - f % PER) % PER), 0.0)

    def column(a, c):
        return jnp.broadcast_to(a[:, c : c + 1], (rows, TILE))

    mix = [[coupling[l, m] for m in range(levels)] for l in range(levels)]

    def prepare(s):
        for p in range(bands):
            got = hal.at[s, p]
            for l in range(levels):
                a1[s, 0, l, padded(p)] = x[s, 0, l, band(p)]
                val = unpack(got, l)
                x[s, 1, l, band(p)] = val
                a1[s, 1, l, padded(p)] = val
            for t in range(2):
                kx, ky, ux = (
                    main[i, s, band(p)] if t == 0 else unpack(got, levels + i) for i in range(3)
                )
                plain = 1.0 - 2.0 * kx - 2.0 * ky
                for l in range(levels):
                    centre[l, s, t, band(p)] = plain + mix[l][l]
                coef[1, s, t, band(p)] = kx + 0.5 * ux
                coef[2, s, t, band(p)] = kx - 0.5 * ux
                kyp[s, t, padded(p)] = ky

    def prepare_late(s):
        for p in range(bands):
            for t in range(2):
                coef[3, s, t, band(p)] = east(*(coef[2, s, k, band(p)] for k in (t, 1 - t)))
                coef[4, s, t, band(p)] = west(*(coef[1, s, k, band(p)] for k in (t, 1 - t)))
            got = hlate.at[s, p]
            wgt[s, 1, band(p)] = unpack(got, 1)
            lev[s, 1, band(p)] = unpack(got, 2)
            info = got[3 // PER]
            base = SLOT * (3 % PER)
            wgt[s, 0, band(p)] = column(info, (base + TILE - HALO) % TILE)
            lev[s, 0, band(p)] = column(info, base)
            for t in range(2):
                ob = main[3, s, band(p)] if t == 0 else unpack(got, 0)
                miss = pick(lambda l: x[s, t, l, band(p)], lev[s, t, band(p)]) - ob
                omt[s, t, band(p)] = 0.5 * (wgt[s, t, band(p)] * miss)

    def east(a, after):
        return pltpu.roll(jnp.where(lane_first, after, a), TILE - 1, 1)

    def west(a, before):
        return pltpu.roll(jnp.where(lane_last, before, a), 1, 1)

    def step(src, dst, s, p, adjoint):
        v = [[src[s, t, l, padded(p)] for l in range(levels)] for t in range(2)]
        for t in range(2):
            ce, cw = (coef[k + 2 * adjoint, s, t, band(p)] for k in (1, 2))
            if adjoint:
                cu, cd = kyp[s, t, padded(p, 1)], kyp[s, t, padded(p, -1)]
            else:
                cr = kyp[s, t, padded(p)]
            for l in range(levels):
                a, o = v[t][l], v[1 - t][l]
                up, down = src[s, t, l, padded(p, 1)], src[s, t, l, padded(p, -1)]
                out = centre[l, s, t, band(p)] * a
                for m in range(levels):
                    if m != l:
                        out += (mix[m][l] if adjoint else mix[l][m]) * v[t][m]
                if adjoint:
                    out += cu * up
                    out += cd * down
                else:
                    out += cr * (up + down)
                out += ce * east(a, o)
                out += cw * west(a, o)
                dst[s, t, l, padded(p)] = out

    def apply(buf, which, adjoint):
        if not which:
            return

        def body(_, carry):
            for src, dst in ((buf, bb), (bb, buf)):
                for s in which:
                    for p in range(bands):
                        step(src, dst, s, p, adjoint)
            return carry

        if len(which) == 1:
            for k in range(STEPS // 2):
                body(k, 0)
        else:
            lax.fori_loop(0, STEPS // 2, body, 0)

    def every(which=(0, 1)):
        return [(t, l, p) for t in which for l in range(levels) for p in range(bands)]

    def squeeze(dst, get):
        for p in range(bands):
            for q in range(xq):
                dst[p, q] = join(
                    [turn(get(l, p), l - q * PER) for l in range(q * PER, min((q + 1) * PER, levels))]
                )

    def widen(dst, src):
        for l in range(levels):
            for p in range(bands):
                dst[1, l, band(p)] = unpack(src.at[p], l)

    def home(src, dst, k, wanted=None):
        for o in range(1, peers):
            _, s, p, dev = peer(o)

            def send():
                remote(
                    src(s, pl.ds(pl.multiple_of(p * rows, rows), rows)),
                    dst.at[:, :, own],
                    6 + k,
                    rsem.at[8 + k],
                    dev,
                ).start()

            if wanted is None:
                send()
            else:
                pl.when(wanted(s))(send)

        def keep():
            mine = src(sme, pl.ds(pl.multiple_of(b * rows, rows), rows))
            pltpu.make_async_copy(mine, dst.at[:, :, own], rsem.at[8 + k]).start()

        if wanted is None:
            keep()
        else:
            pl.when(wanted(sme))(keep)

    def share(src, slots, k):
        def body(t, carry):
            o = lax.rem(t + n - gme, n)

            @pl.when(o > 0)
            def _():
                dev = {"tm": t // bands, "lat": t % bands}
                remote(src, slots.at[o - 1], 11 + k, rsem.at[13 + k], dev).start()

            return carry

        if n > 64:
            lax.fori_loop(0, n, body, 0)
        else:
            for t in range(n):
                body(t, 0)

    def gathered(row, slots, k):
        arrived(slots, rsem.at[13 + k])
        full = jnp.sum(row[...] + jnp.sum(slots[...], axis=0), axis=1, keepdims=True)
        size = float(levels * rows * cols * n)
        return 0.3 / jnp.sqrt(full / size + 1e-6)

    rest = list(range(last))

    prepare(last)
    apply(a1, [last], False)

    @pl.when(jnp.logical_not(last_group))
    def _():
        remote(a1.at[last, 0, :, pl.ds(rows, height)], prior.at[0], 3, rsem.at[5], nxt).start()
        squeeze(psend, lambda l, p: a1[last, 1, l, padded(p)])
        remote(psend, bhal, 3, rsem.at[16], nxt).start()

    for s in rest:
        prepare(s)
    apply(a1, rest, False)

    arrived(main.at[3], rsem.at[15])
    arrived(hlate, rsem.at[18])
    for s in range(per_group):
        prepare_late(s)
    for ref in (a2, a3, a4, a5):
        zero_edges(ref)

    def later_apply(buf):
        @pl.when(jnp.logical_not(last_group))
        def _():
            apply(buf, [last], True)

    def first_adjoint(s, val, t, l, p):
        lam[s + 1, t, l, band(p)] = val
        a2[s, t, l, padded(p)] = val
        a5[s, t, l, padded(p)] = (2.0 - 0.5 * variance[l]) * val

    for s in rest:
        for t, l, p in every():
            val = 0.5 * (x[s + 1, t, l, band(p)] - a1[s, t, l, padded(p)])
            first_adjoint(s, val, t, l, p)
    home(lambda s, r: lam.at[s, 0, :, r], lamh, 0, lambda s: s > 0)
    apply(a2, rest, True)

    while near and len(told) < rounds_for(groups):
        pass_on()
    heard(len(told) - 1)

    def gradient(s, total):
        for t, l, p in every():
            grad = lam[s, t, l, band(p)] - a2[s, t, l, padded(p)]
            grad += jnp.where(lev[s, t, band(p)] == float(l), omt[s, t, band(p)], 0.0)
            gg[s, t, l, band(p)] = grad
            a3[s, t, l, padded(p)] = grad
            if t == 0:
                total += grad * grad
        return total

    def prior_lam():
        @pl.when(first_group)
        def _():
            arrived(prior.at[0], rsem.at[1])
            arrived(bhal, rsem.at[2])

        @pl.when(jnp.logical_not(first_group))
        def _():
            arrived(prior.at[0], rsem.at[5])
            arrived(bhal, rsem.at[16])

        widen(prior, bhal)
        for t, l, p in every():
            lam[0, t, l, band(p)] = 0.5 * (x[0, t, l, band(p)] - prior[t, l, band(p)])

    def send_first():
        @pl.when(jnp.logical_not(first_group))
        def _():
            remote(gg.at[0, 0], gnext.at[0], 4, rsem.at[6], prv).start()
            squeeze(gsend, lambda l, p: gg[0, 1, l, band(p)])
            remote(gsend, ghal, 4, rsem.at[17], prv).start()

    def send_last():
        @pl.when(jnp.logical_not(last_group))
        def _():
            remote(
                a3.at[last, 0, :, pl.ds(rows, height)], prior2, 5, rsem.at[7], nxt
            ).start()

    total = jnp.zeros((rows, TILE), F32)
    if last > 0:
        prior_lam()
        total = gradient(0, total)
        send_first()
    @pl.when(jnp.logical_not(last_group))
    def _():
        arrived(x.at[per_group, 0], rsem.at[3])
        arrived(hnext, rsem.at[4])
        widen(x.at[per_group], hnext)

    has_later = jnp.where(last_group, 0.0, 1.0).astype(F32)
    for t, l, p in every():
        val = (0.5 * has_later) * (x[per_group, t, l, band(p)] - a1[last, t, l, padded(p)])
        first_adjoint(last, val, t, l, p)
    later_apply(a2)

    if last == 0:
        prior_lam()
    for s in range(1 if last > 0 else 0, per_group):
        total = gradient(s, total)
    if last == 0:
        send_first()
    row1[...] = jnp.sum(total, axis=0, keepdims=True)
    share(row1, slots1, 0)
    apply(a3, [last], False)
    send_last()
    home(lambda s, r: lam.at[s, 0, :, r], lamh, 0, lambda s: s == 0)
    home(lambda s, r: gg.at[s, 0, :, r], g1h, 1)
    apply(a3, rest, False)

    for s in rest:
        for t, l, p in every():
            q = gg[s + 1, t, l, band(p)] - a3[s, t, l, padded(p)]
            a4[s, t, l, padded(p)] = q
            if t == 0:
                qm[s + 1, l, band(p)] = q
    home(lambda s, r: qm.at[s, :, r], qh, 2, lambda s: s > 0)

    @pl.when(last_group)
    def _():
        apply(a5, rest, True)

    @pl.when(jnp.logical_not(last_group))
    def _():
        apply(a5, list(range(per_group)), True)

    for s in range(per_group):
        for p in range(bands):
            for l in range(levels):
                plain = (2.0 - 0.5 * variance[l]) * lam[s, 0, l, band(p)] - a5[s, 0, l, padded(p)]
                at_level = lev[s, 0, band(p)] == float(l)
                first[s, l, band(p)] = plain + jnp.where(at_level, 1.5 * omt[s, 0, band(p)], 0.0)

    apply(a4, rest, True)

    @pl.when(jnp.logical_not(last_group))
    def _():
        arrived(gnext.at[0], rsem.at[6])
        arrived(ghal, rsem.at[17])
        widen(gnext, ghal)

    for t, l, p in every():
        q = gnext[t, l, band(p)] - a3[last, t, l, padded(p)]
        a4[last, t, l, padded(p)] = has_later * q
    later_apply(a4)

    @pl.when(jnp.logical_not(first_group))
    def _():
        arrived(prior2, rsem.at[7])

    for _, l, p in every((0,)):
        qm[0, l, band(p)] = gg[0, 0, l, band(p)] - prior2[l, band(p)]


    for s in range(per_group):
        for p in range(bands):
            where = lev[s, 0, band(p)]
            seen = wgt[s, 0, band(p)] * pick(lambda l: gg[s, 0, l, band(p)], where)
            for l in range(levels):
                part = qm[s, l, band(p)] - a4[s, 0, l, padded(p)]
                second[s, l, band(p)] = part + jnp.where(where == float(l), seen, 0.0)

    c1 = gathered(row1, slots1, 0)
    h1 = 0.5 * c1

    total = jnp.zeros((rows, TILE), F32)
    for s in range(per_group):
        for l in range(levels):
            for p in range(bands):
                grad = first[s, l, band(p)] - h1 * second[s, l, band(p)]
                third[s, l, band(p)] = grad
                total += grad * grad
    row2[...] = jnp.sum(total, axis=0, keepdims=True)
    share(row2, slots2, 1)
    home(lambda s, r: qm.at[s, :, r], qh, 2, lambda s: s == 0)
    home(lambda s, r: third.at[s, :, r], g2, 3)

    arrived(g1h, rsem.at[9])
    for l in range(levels):
        xs[l] = xs[l] - c1 * g1h[l]
    for t in range(tiles):
        miss = pick(lambda l: xs[l, :, at(t)], levh[:, at(t)]) - raw[3, :, at(t)]
        om[:, at(t)] += 0.5 * (wgth[:, at(t)] * miss - om[:, at(t)])
    arrived(lamh, rsem.at[8])
    arrived(qh, rsem.at[10])
    for l in range(levels):
        m1[l] = (2.0 - 0.5 * variance[l]) * lamh[l] - h1 * qh[l]

    drain(ssem.at[0], (peers - 1) * (levels + 4 + nq + nl))
    for k in range(4):
        drain(ssem.at[6 + k], (peers - 1) * levels)

    @pl.when(first_group)
    def _():
        if bands > 1:
            drain(ssem.at[1], (bands - 1) * (levels + xq))

    @pl.when(jnp.logical_not(first_group))
    def _():
        drain(ssem.at[2], bands * (levels + xq))
        drain(ssem.at[4], bands * (levels + xq))

    @pl.when(jnp.logical_not(last_group))
    def _():
        drain(ssem.at[3], bands * (levels + xq))
        drain(ssem.at[5], bands * levels)

    arrived(g2, rsem.at[11])
    arrived(slots1, ssem.at[11])
    arrived(slots2, ssem.at[12])
    scale_out[...] = jnp.broadcast_to(gathered(row2, slots2, 1), (1, TILE))


def finish(x, mult, om, grad, scale, state_out, mult_out, om_out, state, sem):
    copies = [
        pltpu.make_async_copy(mult, mult_out.at[0], sem.at[0]),
        pltpu.make_async_copy(om, om_out.at[0], sem.at[1]),
    ]
    for c in copies:
        c.start()
    s = scale[0:1, 0:1]
    for l in range(x.shape[0]):
        state[l] = x[l] - s * grad[l]
    copies.append(pltpu.make_async_copy(state, state_out.at[0], sem.at[2]))
    copies[2].start()
    for c in copies:
        c.wait()


def on_device(subs, bands, *args):
    x = args[0]
    _, levels, rows, cols = x.shape
    n = subs * bands
    tiles = cols // TILE
    per_group = tiles // bands
    if per_group * bands != tiles or subs % per_group:
        raise ValueError("unsupported mesh")
    groups = subs // per_group
    height = bands * rows
    nq = -(-(levels + 3) // PER)
    nl = -(-4 // PER)
    xq = -(-levels // PER)
    dma = pltpu.SemaphoreType.DMA
    vm = lambda *shape: pltpu.VMEM(shape, F32)
    full = vm(levels, rows, cols)
    cell = vm(rows, cols)
    small = pltpu.VMEM((rows, tiles), jnp.int32)
    anywhere = pl.BlockSpec(memory_space=pltpu.HBM)
    vmem = pl.BlockSpec(memory_space=pltpu.VMEM)
    wide = vm(per_group, 2, levels, height + 2 * rows, TILE)
    pair = vm(2, levels, height, TILE)
    held = pl.pallas_call(
        functools.partial(kernel, subs, bands, per_group),
        out_shape=(full, full, cell, full, vm(1, TILE)),
        in_specs=[anywhere] * 10,
        out_specs=(vmem,) * 5,
        scratch_shapes=[
            vm(4, rows, cols),
            pltpu.SMEM((levels, levels), F32),
            pltpu.SMEM((levels,), F32),
            small,
            small,
            cell,
            cell,
            full,
            full,
            full,
            vm(tiles, nq, rows, TILE),
            vm(tiles, nl, rows, TILE),
            vm(per_group, bands, nq, rows, TILE),
            vm(per_group, bands, nl, rows, TILE),
            vm(bands, xq, rows, TILE),
            vm(4, per_group, height, TILE),
            vm(per_group + 1, 2, levels, height, TILE),
            vm(per_group + 1, 2, levels, height, TILE),
            vm(per_group, levels, height, TILE),
            vm(per_group, 2, levels, height, TILE),
            vm(per_group, levels, height, TILE),
            vm(per_group, levels, height, TILE),
            vm(per_group, levels, height, TILE),
            wide,
            wide,
            wide,
            wide,
            wide,
            wide,
            vm(per_group, 2, height + 2 * rows, TILE),
            vm(levels, per_group, 2, height, TILE),
            vm(5, per_group, 2, height, TILE),
            vm(per_group, 2, height, TILE),
            vm(per_group, 2, height, TILE),
            vm(per_group, 2, height, TILE),
            pair,
            vm(levels, height, TILE),
            pair,
            full,
            vm(bands, xq, rows, TILE),
            vm(bands, xq, rows, TILE),
            vm(bands, xq, rows, TILE),
            vm(bands, xq, rows, TILE),
            vm(bands, xq, rows, TILE),
            vm(1, TILE),
            vm(1, TILE),
            vm(n - 1, 1, TILE),
            vm(n - 1, 1, TILE),
            vm((tiles - 1) * (levels + 4 + nq + nl), rows, TILE),
            dma((10,)),
            dma((13,)),
            dma((19,)),
            dma((per_group,)),
            dma((per_group,)),
            pltpu.SemaphoreType.REGULAR((rounds_for(groups),)),
        ],
        compiler_params=pltpu.CompilerParams(
            collective_id=0,
            has_side_effects=True,
        ),
    )(*args)
    return pl.pallas_call(
        finish,
        out_shape=(
            jax.ShapeDtypeStruct(x.shape, F32),
            jax.ShapeDtypeStruct(x.shape, F32),
            jax.ShapeDtypeStruct((1, rows, cols), F32),
        ),
        in_specs=[vmem] * 5,
        out_specs=(anywhere,) * 3,
        scratch_shapes=[full, dma((3,))],
        compiler_params=pltpu.CompilerParams(vmem_limit_bytes=16 << 20),
    )(*held)


def solution(mesh):
    placed = (
        P("tm", None, "lat", None),
        P(None, "lat", None),
        P("tm", "lat", None),
        P("tm", "lat", None),
        P("tm", "lat", None),
        P("tm", "lat", None),
        P(),
        P(),
        P("tm", "lat", None),
        P("tm", "lat", None),
    )
    return jax.shard_map(
        functools.partial(on_device, mesh.shape["tm"], mesh.shape["lat"]),
        mesh=mesh,
        in_specs=placed,
        out_specs=(P("tm", None, "lat", None), P("tm", None, "lat", None), P("tm", "lat", None)),
        check_vma=False,
    )
```
